32 devices in a mesh: groups: 2 (over y), depth: 4 (over z), cols: 2 (over x), heads: 2 (over core).
Axes of the slice: x: 2, y: 2, z: 4, core: 2. Of those that a mesh axis runs over, the one named last changes fastest.
Arguments:
- alignment: bfloat16 [64, 256, 768], P(('groups', 'depth'), 'cols'), parts along dimension 0, may hold values from -6 to 6
- norm_gain: float32 [768], replicated, may hold values from 0.25 to 1.75
- w_query: bfloat16 [768, 768], P(None, 'heads'), may hold values from -1 to 1
- w_key: bfloat16 [768, 768], P(None, 'heads'), may hold values from -2 to 2
- w_value: bfloat16 [768, 768], P(None, 'heads'), may hold values from -0.21875 to 0.21875
- w_out: bfloat16 [768, 768], P(None, 'heads'), may hold values from -0.21875 to 0.21875
- row_mask: int32 [64], P(('groups', 'depth')), parts along dimension 0, may hold values 0 or 1
- col_valid: int32 [512], P(('groups', 'cols')), parts along dimension 0, may hold values 0 or 1
Outputs:
- attended: bfloat16 [64, 256, 768], P(('groups', 'depth'), 'cols', 'heads'), parts along dimension 0
The draws below stay inside these ranges and needn't reach their ends.
There are 2 independent parts, one for each index of `groups`. The reference program is written for one: setup_inputs(seed, part) draws one part's arguments, and reference() takes and returns one part's arrays. A program takes and returns all parts, laid end to end along the dimension named above; an argument that names none is the same for every part. Nothing has to cross between parts.
Inputs may be any that keep to these rules, and one draw needn't show every extreme that they name: `col_valid`: some column of every family is valid. `row_mask`: some row of every family is real.
All inputs are finite; a program needn't handle non-finite values. No bound on the sum of `row_mask` or of `col_valid` on one device may be relied on, other than what follows from the above.
Results may differ from the reference program's by a relative error of at most 0.009.
Values may be sent and summed in bfloat16 or wider, within the bound.
No kernel may reach another device: no remote copies, remote signals or barrier semaphores. Data moves between devices by JAX's collectives and lax.ppermute only.
A program may use at most 64 MiB of HBM per device.

```python
import jax
import jax.numpy as jnp
from jax import lax

D = 768
HEADS = 12
HEAD_DIM = 64
ROWS = 32
C = 256


def weight_pair(key):
    first = jax.random.normal(jax.random.fold_in(key, 101), (D, D), jnp.float32)
    second = jax.random.normal(jax.random.fold_in(key, 102), (D, D), jnp.float32)
    factor = D ** (-0.5)
    return (jnp.clip(first, -4.0, 4.0) * factor, jnp.clip(second, -4.0, 4.0) * factor)


def draw_w_query(key, part):
    query_part, other_part = weight_pair(key)
    return query_part.astype(jnp.bfloat16)


def draw_w_key(key, part):
    query_part, other_part = weight_pair(key)
    result = other_part
    return result.astype(jnp.bfloat16)


def draw_alignment(key, part):
    base = jnp.clip(jax.random.normal(jax.random.fold_in(key, 201), (ROWS, C, D), jnp.float32), -6.0, 6.0)
    return base.astype(jnp.bfloat16)


def touch_ends(entries, stream_key, smallest, high):
    place = [jax.random.randint(jax.random.fold_in(stream_key, axis), (), 0, length) for axis, length in enumerate(entries.shape)]
    longest = entries.shape.index(max(entries.shape))
    next_to = place[:longest] + [(place[longest] + 1) % entries.shape[longest]] + place[longest + 1:]
    return entries.at[tuple(place)].set(smallest).at[tuple(next_to)].set(high)


def block_scale(stream_key, extent, split, smallest, high):
    def one(axis_at, shards_of):
        heights = jax.random.uniform(jax.random.fold_in(jax.random.fold_in(stream_key, 6), axis_at), (shards_of,), jnp.float32, smallest / len(split), high / len(split))
        return jnp.repeat(jnp.exp(heights), extent[axis_at] // shards_of).reshape((-1,) + (1,) * (len(extent) - axis_at - 1))

    gain = one(*split[0])
    for cut in split[1:]:
        gain = gain * one(*cut)
    return gain


def normal_values(key, extent, deviation, bound, split=(), kind=jnp.bfloat16):
    drawn = deviation * jax.random.normal(key, extent, jnp.float32)
    if split:
        drawn = drawn * block_scale(key, extent, split, -0.22, 0.18)
    return jnp.clip(drawn, -bound, bound).astype(kind)


def setup_inputs(seed: int = 0, part: int = 0) -> dict:
    seeds = jax.random.split(jax.random.key(seed), 9)
    own_keys = jax.random.split(jax.random.fold_in(seeds[8], part), 9)
    alignment = draw_alignment(jax.random.fold_in(jax.random.fold_in(seeds[8], part), 71), part)
    norm_gain = jnp.clip(1.0 + 0.15 * jax.random.normal(seeds[1], (D,), jnp.float32), 0.25, 1.75)
    w_query = draw_w_query(jax.random.fold_in(seeds[8], 71), part)
    w_key = draw_w_key(jax.random.fold_in(seeds[8], 71), part)
    w_value = normal_values(seeds[4], (D, D), D ** -0.5, 0.21875, ((1, 2),))
    w_out = normal_values(seeds[5], (D, D), D ** -0.5, 0.21875, ((1, 2),))
    row_mask = touch_ends((jax.random.randint(own_keys[6], (ROWS,), 0, 4) < 3).astype(jnp.int32), jax.random.fold_in(own_keys[6], 1), 0, 1)
    col_valid = touch_ends((jax.random.randint(own_keys[7], (C,), 0, 8) < 7).astype(jnp.int32), jax.random.fold_in(own_keys[7], 1), 0, 1)
    return {"alignment": alignment, "norm_gain": norm_gain, "w_query": w_query, "w_key": w_key, "w_value": w_value, "w_out": w_out, "row_mask": row_mask, "col_valid": col_valid}


def reference(alignment, norm_gain, w_query, w_key, w_value, w_out, row_mask, col_valid):
    values_f = alignment.astype(jnp.float32)
    average = lax.optimization_barrier(jnp.mean(values_f, axis=-1, keepdims=True))
    centred = values_f - average
    spread = lax.optimization_barrier(jnp.mean(centred * centred, axis=-1, keepdims=True))
    normed = (centred * lax.rsqrt(spread + 1e-05) * norm_gain).astype(jnp.bfloat16)
    flattened = normed.reshape(-1, D)
    alive_rows = row_mask.astype(jnp.float32)
    count = jnp.sum(alive_rows)
    row_scale = jnp.repeat(alive_rows, C)[:, None]
    queries = (jnp.dot(flattened, w_query, preferred_element_type=jnp.float32) * row_scale).astype(jnp.bfloat16)
    key_rows = jnp.dot(flattened, w_key, preferred_element_type=jnp.float32).astype(jnp.bfloat16)
    value_rows = jnp.dot(flattened, w_value, preferred_element_type=jnp.float32).astype(jnp.bfloat16)
    queries = queries.reshape(ROWS, C, HEADS, HEAD_DIM).astype(jnp.float32)
    key_rows = key_rows.reshape(ROWS, C, HEADS, HEAD_DIM).astype(jnp.float32)
    value_rows = value_rows.reshape(ROWS, C, HEADS, HEAD_DIM).astype(jnp.float32)
    logits = jnp.einsum('rihe,rjhe->hij', queries, key_rows)
    scaled = logits * lax.rsqrt(jnp.float32(HEAD_DIM) * count)
    valid_cols = col_valid == 1
    scaled = jnp.where(valid_cols[None, None, :], scaled, -1e+30)
    top = lax.optimization_barrier(jnp.max(scaled, axis=-1, keepdims=True))
    expo = jnp.where(valid_cols[None, None, :], jnp.exp(scaled - top), 0.0)
    probs = (expo / lax.optimization_barrier(jnp.sum(expo, axis=-1, keepdims=True))).astype(jnp.bfloat16)
    heads_out = jnp.einsum('hij,rjhe->rihe', probs.astype(jnp.float32), value_rows)
    heads_out = heads_out.astype(jnp.bfloat16).reshape(-1, D)
    attended = jnp.dot(heads_out, w_out, preferred_element_type=jnp.float32) * row_scale
    return attended.astype(jnp.bfloat16).reshape(ROWS, C, D)
```

```python
import functools

import jax
import jax.numpy as jnp
from jax import lax
from jax.experimental import pallas as pl
from jax.experimental.pallas import tpu as pltpu
from jax.sharding import PartitionSpec as P

HEADS = 12
LANES = 128
CHUNKS = 2
MAX_DIRECT = 8


VMEM = pltpu.MemorySpace.VMEM
SMEM = pltpu.MemorySpace.SMEM


def from_behind(value, axis, steps):
    count = lax.axis_size(axis)
    pairs = [(source, (source + steps) % count) for source in range(count)]
    return lax.ppermute(value, axis, pairs)


def spec(space=VMEM):
    return pl.BlockSpec(memory_space=space)


def call(kernel, out_shape, in_specs, scratch=(), flops=0, name=None):
    single = not isinstance(out_shape, (list, tuple))
    shapes = [out_shape] if single else list(out_shape)
    nbytes = sum(s.size * s.dtype.itemsize for s in shapes)
    fn = pl.pallas_call(
        kernel,
        out_shape=shapes,
        in_specs=in_specs,
        out_specs=[spec() for _ in shapes],
        scratch_shapes=list(scratch),
        cost_estimate=pl.CostEstimate(flops=flops, transcendentals=0, bytes_accessed=2 * nbytes),
        name=name,
    )

    def run(*args):
        out = fn(*args)
        return out[0] if single else out

    return run


def normed_rows(rows, gain):
    values_f = rows.astype(jnp.float32)
    average = jnp.mean(values_f, axis=-1, keepdims=True)
    centred = values_f - average
    spread = jnp.mean(centred * centred, axis=-1, keepdims=True)
    return (centred * lax.rsqrt(spread + 1e-05) * gain).astype(jnp.bfloat16)


def dot(left, right):
    return jnp.dot(left, right, preferred_element_type=jnp.float32)


def dot_t(left, right):
    return lax.dot_general(left, right, (((1,), (1,)), ((), ())), preferred_element_type=jnp.float32)


def side_by_side(block, rows, cols, begin):
    pieces = [block[r * cols : (r + 1) * cols, begin : begin + LANES] for r in range(rows)]
    return jnp.concatenate(pieces, axis=1) if rows > 1 else pieces[0]


def write_shards(total, shards, shard_cols, depth_index, count):
    heads = total.shape[0]
    for k, shard in enumerate(shards):
        begin = pl.multiple_of(lax.rem(depth_index + k, count) * shard_cols, shard_cols)
        for head in range(heads):
            shard[head * shard_cols : (head + 1) * shard_cols, :] = total[
                head, pl.ds(begin, shard_cols), :
            ]


def own_kernel(place, live, rows_in, gain, w_query, w_key, *rest, groups, shard_cols, shard_count):
    normed_out, query_out = rest[0], rest[1]
    shards = rest[2 : 2 + shard_count]
    keys, total = rest[2 + shard_count :]
    rows_here, cols, width = rows_in.shape
    size = rows_here // groups
    pairs = query_out.shape[1]
    low = lax.broadcasted_iota(jnp.int32, (cols, LANES), 1) < LANES // 2
    zero = jnp.zeros((cols, LANES), jnp.bfloat16)
    for g in range(groups):
        normed = normed_rows(rows_in[g * size : (g + 1) * size].reshape(size * cols, width), gain[...])
        normed_out[g] = normed
        query = dot(normed, w_query[...])
        key = dot(normed, w_key[...]).astype(jnp.bfloat16)
        for r in range(size):
            scale = live[g * size + r].astype(jnp.float32)
            piece = (query[r * cols : (r + 1) * cols] * scale).astype(jnp.bfloat16)
            for p in range(pairs):
                both = piece[:, p * LANES : (p + 1) * LANES]
                at = pl.ds(r * LANES, LANES)
                query_out[g, p, 0:cols, at] = jnp.where(low, both, zero)
                query_out[g, p, cols : 2 * cols, at] = jnp.where(low, zero, both)
        for p in range(pairs):
            keys[g, p] = side_by_side(key, size, cols, p * LANES)
    for p in range(pairs):
        score = dot_t(query_out[0, p], keys[0, p])
        for g in range(1, groups):
            score = score + dot_t(query_out[g, p], keys[g, p])
        total[2 * p] = score[:cols]
        total[2 * p + 1] = score[cols:]
    write_shards(total, shards, shard_cols, place[0], shard_count)
    real = jnp.float32(0)
    for r in range(rows_here):
        real = real + live[r].astype(jnp.float32)
    for shard in shards:
        shard[2 * pairs * shard_cols :, :] = jnp.full((8, LANES), real, jnp.float32)


def value_kernel(normed, w_value, values, *, cols):
    groups, pairs = values.shape[0], values.shape[1]
    for g in range(groups):
        value = dot(normed[g], w_value[...]).astype(jnp.bfloat16)
        for p in range(pairs):
            values[g, p] = side_by_side(value, value.shape[0] // cols, cols, p * LANES)


def remote_kernel(place, *rest, cores, chunks, chunk, first, last, shard_cols, shard_count):
    parts = rest[:cores]
    gain, w_key, query = rest[cores : cores + 3]
    rest = rest[cores + 3 :]
    if not first:
        before, rest = rest[0], rest[1:]
    normed_out, rest = rest[0], rest[1:]
    size, cols, width = parts[0].shape
    pairs = query.shape[1]
    keys = []
    for k in range(cores):
        normed = normed_rows(parts[k][...].reshape(size * cols, width), gain[...])
        normed_out[k] = normed
        keys.append(dot(normed, w_key[...]).astype(jnp.bfloat16))
    for p in range(pairs):
        score = None if first else before[p]
        for k in range(cores):
            group = lax.rem(place[1] + cores - k, cores) * chunks + chunk
            part = dot_t(query[group, p], side_by_side(keys[k], size, cols, p * LANES))
            score = part if score is None else score + part
        if last:
            total = rest[shard_count]
            total[2 * p] = score[:cols]
            total[2 * p + 1] = score[cols:]
        else:
            rest[0][p] = score
    if last:
        write_shards(rest[shard_count], rest[:shard_count], shard_cols, place[0], shard_count)


def soft_kernel(valid, *rest, tiles, shard_count, head_width):
    probs = rest[-1]
    rows, cols = probs.shape[0], rest[0].shape[1]
    totals = []
    for t in range(tiles):
        pieces = rest[t * shard_count : (t + 1) * shard_count]
        total = pieces[0][...]
        for piece in pieces[1:]:
            total = total + piece[...]
        totals.append(total)
    real = totals[0][rows : rows + 1, 0:1]
    factor = lax.rsqrt(jnp.float32(head_width) * real)
    scaled, tops = [], []
    for t in range(tiles):
        mask = valid[:, t * cols : (t + 1) * cols] > 0.5
        part = jnp.where(mask, totals[t][:rows] * factor, -1e30)
        scaled.append(part)
        tops.append(jnp.max(part, axis=-1, keepdims=True))
    top = functools.reduce(jnp.maximum, tops)
    expos, sums = [], []
    for t in range(tiles):
        mask = valid[:, t * cols : (t + 1) * cols] > 0.5
        expo = jnp.where(mask, jnp.exp(scaled[t] - top), 0.0)
        expos.append(expo)
        sums.append(jnp.sum(expo, axis=-1, keepdims=True))
    whole = functools.reduce(jnp.add, sums)
    for t in range(tiles):
        probs[:, t * cols : (t + 1) * cols] = (expos[t] / whole).astype(jnp.bfloat16)


def mix_kernel(place, *rest, shard_count, offsets, cores, chunks):
    shards = rest[:shard_count]
    values = rest[shard_count]
    remote = rest[shard_count + 1 : shard_count + 1 + offsets * chunks]
    out, probs = rest[shard_count + 1 + offsets * chunks :]
    groups, pairs, cols, _ = values.shape
    size = values.shape[3] // LANES
    shard_cols = cols // shard_count
    for k, shard in enumerate(shards):
        source = lax.rem(place[0] + shard_count - k, shard_count)
        for head in range(2 * pairs):
            begin = pl.multiple_of((head % 2) * cols + source * shard_cols, shard_cols)
            probs[head // 2, pl.ds(begin, shard_cols), :] = shard[
                head * shard_cols : (head + 1) * shard_cols, :
            ]
    lane = lax.broadcasted_iota(jnp.int32, (cols, LANES * size), 1)
    low = lax.rem(lane, LANES) < LANES // 2
    for k in range(cores):
        for c in range(chunks):
            group = lax.rem(place[1] + cores - k, cores) * chunks + c
            for p in range(pairs):
                blocks = [values[group, p]]
                blocks += [remote[o * chunks + c][k, p] for o in range(offsets)]
                both = jnp.concatenate(blocks, axis=0) if offsets else blocks[0]
                mixed = dot(probs[p], both)
                picked = jnp.where(low, mixed[:cols], mixed[cols:]).astype(jnp.bfloat16)
                for r in range(size):
                    out[group * size + r, :, p * LANES : (p + 1) * LANES] = picked[
                        :, r * LANES : (r + 1) * LANES
                    ]


def out_kernel(place, live, *rest, cores):
    parts = rest[:cores]
    w_out, out = rest[cores], rest[cores + 1]
    rows_here, cols, local = parts[0].shape
    step = min(rows_here, 2)
    for begin in range(0, rows_here, step):
        total = None
        for k in range(cores):
            source = lax.rem(place[1] + cores - k, cores)
            block = parts[k][begin : begin + step].reshape(step * cols, local)
            part = dot(block, w_out[pl.ds(pl.multiple_of(source * local, local), local), :])
            total = part if total is None else total + part
        for r in range(step):
            scale = live[begin + r].astype(jnp.float32)
            out[begin + r] = (total[r * cols : (r + 1) * cols] * scale).astype(jnp.bfloat16)


def on_device(alignment, norm_gain, w_query, w_key, w_value, w_out, row_mask, col_valid):
    rows_here, cols_here, width = alignment.shape
    local_width = w_query.shape[1]
    head_width = width // HEADS
    local_heads = local_width // head_width
    pairs = local_width // LANES
    blocks = lax.axis_size("cols")
    depth = lax.axis_size("depth")
    cores = lax.axis_size("heads")
    core = lax.axis_index("heads")
    place = jnp.stack([lax.axis_index("depth"), core]).astype(jnp.int32)
    share = rows_here // cores
    size = share // CHUNKS
    groups = cores * CHUNKS
    direct = depth <= MAX_DIRECT and cols_here % (16 * depth) == 0
    shard_count = depth if direct else 1
    shard_cols = cols_here // shard_count
    shard_rows = local_heads * shard_cols
    bf16, f32 = jnp.bfloat16, jnp.float32
    shape = jax.ShapeDtypeStruct
    gain = norm_gain[None, :]

    arrived = {}
    valid_tiles = [col_valid.astype(bf16)[None, :]]
    for offset in range(1, blocks):
        for c in range(CHUNKS):
            mine = lax.dynamic_slice_in_dim(alignment, core * share + c * size, size, 0)
            mine = from_behind(mine, "cols", offset)
            arrived[offset, c] = [mine] + [from_behind(mine, "heads", k) for k in range(1, cores)]
        valid_tiles.append(from_behind(valid_tiles[0], "cols", offset))
    valid = jnp.concatenate(valid_tiles, axis=1).astype(f32)

    own = call(
        functools.partial(
            own_kernel, groups=groups, shard_cols=shard_cols, shard_count=shard_count
        ),
        [
            shape((groups, size * cols_here, width), bf16),
            shape((groups, pairs, 2 * cols_here, size * LANES), bf16),
        ]
        + [shape((shard_rows + 8, cols_here), f32)] * shard_count,
        [spec(SMEM), spec(SMEM)] + [spec()] * 4,
        [
            pltpu.VMEM((groups, pairs, cols_here, size * LANES), bf16),
            pltpu.VMEM((local_heads, cols_here, cols_here), f32),
        ],
        flops=4 * rows_here * cols_here * width * local_width,
        name="own",
    )(place, row_mask, alignment, gain, w_query, w_key)
    normed, query, own_shards = own[0], own[1], own[2:]

    def exchange(shards):
        return [shards[0]] + [from_behind(shards[k], "depth", k) for k in range(1, len(shards))]

    own_shards = exchange(own_shards)

    def project(rows):
        return call(
            functools.partial(value_kernel, cols=cols_here),
            shape((rows.shape[0], pairs, cols_here, size * LANES), bf16),
            [spec()] * 2,
            flops=2 * rows.size * local_width,
            name="values",
        )(rows, w_value)

    values = project(normed)
    tiles, remote_values = [own_shards], []
    for offset in range(1, blocks):
        before = []
        for c in range(CHUNKS):
            last = c + 1 == CHUNKS
            outs = [shape((cores, size * cols_here, width), bf16)]
            if last:
                outs += [shape((shard_rows, cols_here), f32)] * shard_count
                scratch = [pltpu.VMEM((local_heads, cols_here, cols_here), f32)]
            else:
                outs += [shape((pairs, 2 * cols_here, cols_here), f32)]
                scratch = []
            result = call(
                functools.partial(
                    remote_kernel,
                    cores=cores,
                    chunks=CHUNKS,
                    chunk=c,
                    first=c == 0,
                    last=last,
                    shard_cols=shard_cols,
                    shard_count=shard_count,
                ),
                outs,
                [spec(SMEM)] + [spec()] * (cores + 3 + len(before)),
                scratch,
                flops=2 * cores * size * cols_here * width * local_width,
                name="remote",
            )(place, *arrived[offset, c], gain, w_key, query, *before)
            if last:
                tiles.append(exchange(result[1:]))
            else:
                before = [result[1]]
            remote_values.append(project(result[0]))

    if direct:
        probs = call(
            functools.partial(
                soft_kernel, tiles=blocks, shard_count=shard_count, head_width=head_width
            ),
            shape((shard_rows, blocks * cols_here), bf16),
            [spec()] * (1 + blocks * shard_count),
            flops=1000000,
            name="soft",
        )(valid, *[piece for tile in tiles for piece in tile])
        shards = [probs] + [from_behind(probs, "depth", k) for k in range(1, shard_count)]
    else:
        count = lax.psum(jnp.sum(row_mask.astype(f32)), "depth")
        logits = jnp.concatenate(
            [tile[0][:shard_rows].reshape(local_heads, cols_here, cols_here) for tile in tiles], axis=2
        )
        part = lax.psum_scatter(logits, "depth", scatter_dimension=1, tiled=True)
        mask = valid[None] > 0.5
        scaled = jnp.where(mask, part * lax.rsqrt(f32(head_width) * count), -1e30)
        expo = jnp.where(mask, jnp.exp(scaled - jnp.max(scaled, axis=-1, keepdims=True)), 0.0)
        probs = (expo / jnp.sum(expo, axis=-1, keepdims=True)).astype(bf16)
        probs = lax.all_gather(probs, "depth", axis=1, tiled=True)
        shards = [probs.reshape(shard_rows, blocks * cols_here)]

    heads_out = call(
        functools.partial(
            mix_kernel,
            shard_count=shard_count,
            offsets=blocks - 1,
            cores=cores,
            chunks=CHUNKS,
        ),
        shape((rows_here, cols_here, local_width), bf16),
        [spec(SMEM)] + [spec()] * (shard_count + 1 + len(remote_values)),
        [pltpu.VMEM((pairs, 2 * cols_here, blocks * cols_here), bf16)],
        flops=4 * rows_here * cols_here * blocks * cols_here * local_width,
        name="mix",
    )(place, *shards, values, *remote_values)
    parts = [heads_out] + [from_behind(heads_out, "heads", k) for k in range(1, cores)]
    return call(
        functools.partial(out_kernel, cores=cores),
        shape((rows_here, cols_here, local_width), bf16),
        [spec(SMEM), spec(SMEM)] + [spec()] * (cores + 1),
        flops=2 * rows_here * cols_here * width * local_width,
        name="project",
    )(place, row_mask, *parts, w_out)


def solution(mesh):
    in_specs = (
        P(("groups", "depth"), "cols", None),
        P(),
        P(None, "heads"),
        P(None, "heads"),
        P(None, "heads"),
        P(None, "heads"),
        P(("groups", "depth")),
        P(("groups", "cols")),
    )
    out_specs = P(("groups", "depth"), "cols", "heads")
    return jax.shard_map(
        on_device, mesh=mesh, in_specs=in_specs, out_specs=out_specs, check_vma=False
    )
```

```python
import functools

import jax
import jax.numpy as jnp
from jax import lax
from jax.experimental import pallas as pl
from jax.experimental.pallas import tpu as pltpu
from jax.sharding import PartitionSpec as P

HEADS = 12
LANES = 128
CHUNKS = 2
MAX_DIRECT = 8
LIMIT = 16 << 20


VMEM = pltpu.MemorySpace.VMEM
SMEM = pltpu.MemorySpace.SMEM


def from_behind(value, axis, steps):
    count = lax.axis_size(axis)
    pairs = [(source, (source + steps) % count) for source in range(count)]
    return lax.ppermute(value, axis, pairs)


def spec(space=VMEM):
    return pl.BlockSpec(memory_space=space)


def call(kernel, out_shape, in_specs, scratch=(), flops=0, out_block=None):
    single = not isinstance(out_shape, (list, tuple))
    shapes = [out_shape] if single else list(out_shape)
    nbytes = sum(s.size * s.dtype.itemsize for s in shapes)
    grid, out_specs = (), [spec() for _ in shapes]
    if out_block is not None:
        grid = (shapes[0].shape[0] // out_block[0],)
        out_specs = [pl.BlockSpec(out_block, lambda i: (i, 0, 0))]
    else:
        shapes = [pltpu.VMEM(s.shape, s.dtype) for s in shapes]
    fn = pl.pallas_call(
        kernel,
        out_shape=shapes,
        grid=grid,
        in_specs=in_specs,
        out_specs=out_specs,
        scratch_shapes=list(scratch),
        compiler_params=pltpu.CompilerParams(vmem_limit_bytes=LIMIT),
        cost_estimate=pl.CostEstimate(flops=flops, transcendentals=0, bytes_accessed=2 * nbytes),
    )

    def run(*args):
        args = [
            pltpu.with_memory_space_constraint(arg, VMEM) if block.memory_space == VMEM else arg
            for arg, block in zip(args, in_specs, strict=True)
        ]
        out = fn(*args)
        return out[0] if single else out

    return run


def normed_rows(rows, gain):
    values_f = rows.astype(jnp.float32)
    average = jnp.mean(values_f, axis=-1, keepdims=True)
    centred = values_f - average
    spread = jnp.mean(centred * centred, axis=-1, keepdims=True)
    return (centred * lax.rsqrt(spread + 1e-05) * gain).astype(jnp.bfloat16)


def dot(left, right):
    return jnp.dot(left, right, preferred_element_type=jnp.float32)


def dot_t(left, right):
    return lax.dot_general(left, right, (((1,), (1,)), ((), ())), preferred_element_type=jnp.float32)


def side_by_side(block, rows, cols, begin):
    pieces = [block[r * cols : (r + 1) * cols, begin : begin + LANES] for r in range(rows)]
    return jnp.concatenate(pieces, axis=1) if rows > 1 else pieces[0]


def write_shards(total, shards, shard_cols, depth_index, count):
    heads = total.shape[0]
    for k, shard in enumerate(shards):
        begin = pl.multiple_of(lax.rem(depth_index + k, count) * shard_cols, shard_cols)
        for head in range(heads):
            shard[head * shard_cols : (head + 1) * shard_cols, :] = total[
                head, pl.ds(begin, shard_cols), :
            ]


def own_kernel(place, live, rows_in, gain, w_query, w_key, *rest, groups, shard_cols, shard_count):
    normed_out, query_out = rest[0], rest[1]
    shards = rest[2 : 2 + shard_count]
    keys, total = rest[2 + shard_count :]
    rows_here, cols, width = rows_in.shape
    size = rows_here // groups
    pairs = query_out.shape[1]
    low = lax.broadcasted_iota(jnp.int32, (cols, LANES), 1) < LANES // 2
    zero = jnp.zeros((cols, LANES), jnp.bfloat16)
    for g in range(groups):
        normed = normed_rows(rows_in[g * size : (g + 1) * size].reshape(size * cols, width), gain[...])
        normed_out[g] = normed
        query = dot(normed, w_query[...])
        key = dot(normed, w_key[...]).astype(jnp.bfloat16)
        for r in range(size):
            scale = live[g * size + r].astype(jnp.float32)
            piece = (query[r * cols : (r + 1) * cols] * scale).astype(jnp.bfloat16)
            for p in range(pairs):
                both = piece[:, p * LANES : (p + 1) * LANES]
                at = pl.ds(r * LANES, LANES)
                query_out[g, p, 0:cols, at] = jnp.where(low, both, zero)
                query_out[g, p, cols : 2 * cols, at] = jnp.where(low, zero, both)
        for p in range(pairs):
            keys[g, p] = side_by_side(key, size, cols, p * LANES)
    for p in range(pairs):
        score = dot_t(query_out[0, p], keys[0, p])
        for g in range(1, groups):
            score = score + dot_t(query_out[g, p], keys[g, p])
        total[2 * p] = score[:cols]
        total[2 * p + 1] = score[cols:]
    write_shards(total, shards, shard_cols, place[0], shard_count)
    real = jnp.float32(0)
    for r in range(rows_here):
        real = real + live[r].astype(jnp.float32)
    for shard in shards:
        shard[2 * pairs * shard_cols :, :] = jnp.full((8, LANES), real, jnp.float32)


def value_kernel(normed, w_value, values, *, cols):
    groups, pairs = values.shape[0], values.shape[1]
    for g in range(groups):
        value = dot(normed[g], w_value[...]).astype(jnp.bfloat16)
        for p in range(pairs):
            values[g, p] = side_by_side(value, value.shape[0] // cols, cols, p * LANES)


def remote_kernel(place, *rest, cores, chunks, chunk, first, last, shard_cols, shard_count):
    parts = rest[:cores]
    gain, w_key, query = rest[cores : cores + 3]
    rest = rest[cores + 3 :]
    if not first:
        before, rest = rest[0], rest[1:]
    normed_out, rest = rest[0], rest[1:]
    size, cols, width = parts[0].shape
    pairs = query.shape[1]
    keys = []
    for k in range(cores):
        normed = normed_rows(parts[k][...].reshape(size * cols, width), gain[...])
        normed_out[k] = normed
        keys.append(dot(normed, w_key[...]).astype(jnp.bfloat16))
    for p in range(pairs):
        score = None if first else before[p]
        for k in range(cores):
            group = lax.rem(place[1] + cores - k, cores) * chunks + chunk
            part = dot_t(query[group, p], side_by_side(keys[k], size, cols, p * LANES))
            score = part if score is None else score + part
        if last:
            total = rest[shard_count]
            total[2 * p] = score[:cols]
            total[2 * p + 1] = score[cols:]
        else:
            rest[0][p] = score
    if last:
        write_shards(rest[shard_count], rest[:shard_count], shard_cols, place[0], shard_count)


def soft_kernel(valid, *rest, tiles, shard_count, head_width):
    probs = rest[-1]
    rows, cols = probs.shape[0], rest[0].shape[1]
    totals = []
    for t in range(tiles):
        pieces = rest[t * shard_count : (t + 1) * shard_count]
        total = pieces[0][...]
        for piece in pieces[1:]:
            total = total + piece[...]
        totals.append(total)
    real = totals[0][rows : rows + 1, 0:1]
    factor = lax.rsqrt(jnp.float32(head_width) * real)
    scaled, tops = [], []
    for t in range(tiles):
        mask = valid[:, t * cols : (t + 1) * cols] > 0.5
        part = jnp.where(mask, totals[t][:rows] * factor, -1e30)
        scaled.append(part)
        tops.append(jnp.max(part, axis=-1, keepdims=True))
    top = functools.reduce(jnp.maximum, tops)
    expos, sums = [], []
    for t in range(tiles):
        mask = valid[:, t * cols : (t + 1) * cols] > 0.5
        expo = jnp.where(mask, jnp.exp(scaled[t] - top), 0.0)
        expos.append(expo)
        sums.append(jnp.sum(expo, axis=-1, keepdims=True))
    whole = functools.reduce(jnp.add, sums)
    for t in range(tiles):
        probs[:, t * cols : (t + 1) * cols] = (expos[t] / whole).astype(jnp.bfloat16)


def mix_kernel(place, *rest, shard_count, offsets, cores, chunks):
    shards = rest[:shard_count]
    values = rest[shard_count]
    remote = rest[shard_count + 1 : shard_count + 1 + offsets * chunks]
    out, probs = rest[shard_count + 1 + offsets * chunks :]
    _, pairs, cols, _ = values.shape
    size = values.shape[3] // LANES
    shard_cols = cols // shard_count
    for k, shard in enumerate(shards):
        source = lax.rem(place[0] + shard_count - k, shard_count)
        for head in range(2 * pairs):
            begin = pl.multiple_of((head % 2) * cols + source * shard_cols, shard_cols)
            probs[head // 2, pl.ds(begin, shard_cols), :] = shard[
                head * shard_cols : (head + 1) * shard_cols, :
            ]
    lane = lax.broadcasted_iota(jnp.int32, (cols, LANES * size), 1)
    low = lax.rem(lane, LANES) < LANES // 2
    for k in range(cores):
        for c in range(chunks):
            group = lax.rem(place[1] + cores - k, cores) * chunks + c
            for p in range(pairs):
                blocks = [values[group, p]]
                blocks += [remote[o * chunks + c][k, p] for o in range(offsets)]
                both = jnp.concatenate(blocks, axis=0) if offsets else blocks[0]
                mixed = dot(probs[p], both)
                picked = jnp.where(low, mixed[:cols], mixed[cols:]).astype(jnp.bfloat16)
                for r in range(size):
                    out[group * size + r, :, p * LANES : (p + 1) * LANES] = picked[
                        :, r * LANES : (r + 1) * LANES
                    ]


def out_kernel(place, live, *rest, cores):
    parts = rest[:cores]
    w_out, out = rest[cores], rest[cores + 1]
    step, cols, _ = out.shape
    local = parts[0].shape[2]
    begin = pl.program_id(0) * step
    total = None
    for k in range(cores):
        source = lax.rem(place[1] + cores - k, cores)
        block = parts[k][pl.ds(begin, step)].reshape(step * cols, local)
        part = dot(block, w_out[pl.ds(pl.multiple_of(source * local, local), local), :])
        total = part if total is None else total + part
    for r in range(step):
        scale = live[begin + r].astype(jnp.float32)
        out[r] = (total[r * cols : (r + 1) * cols] * scale).astype(jnp.bfloat16)


def on_device(alignment, norm_gain, w_query, w_key, w_value, w_out, row_mask, col_valid):
    rows_here, cols_here, width = alignment.shape
    local_width = w_query.shape[1]
    head_width = width // HEADS
    local_heads = local_width // head_width
    pairs = local_width // LANES
    blocks = lax.axis_size("cols")
    depth = lax.axis_size("depth")
    cores = lax.axis_size("heads")
    core = lax.axis_index("heads")
    place = jnp.stack([lax.axis_index("depth"), core]).astype(jnp.int32)
    share = rows_here // cores
    size = share // CHUNKS
    groups = cores * CHUNKS
    direct = depth <= MAX_DIRECT and cols_here % (16 * depth) == 0
    shard_count = depth if direct else 1
    shard_cols = cols_here // shard_count
    shard_rows = local_heads * shard_cols
    bf16, f32 = jnp.bfloat16, jnp.float32
    shape = jax.ShapeDtypeStruct
    gain = norm_gain[None, :]

    arrived = {}
    valid_tiles = [col_valid.astype(bf16)[None, :]]
    for offset in range(1, blocks):
        for c in range(CHUNKS):
            mine = lax.dynamic_slice_in_dim(alignment, core * share + c * size, size, 0)
            mine = from_behind(mine, "cols", offset)
            arrived[offset, c] = [mine] + [from_behind(mine, "heads", k) for k in range(1, cores)]
        valid_tiles.append(from_behind(valid_tiles[0], "cols", offset))
    valid = jnp.concatenate(valid_tiles, axis=1).astype(f32)

    own = call(
        functools.partial(
            own_kernel, groups=groups, shard_cols=shard_cols, shard_count=shard_count
        ),
        [
            shape((groups, size * cols_here, width), bf16),
            shape((groups, pairs, 2 * cols_here, size * LANES), bf16),
        ]
        + [shape((shard_rows + 8, cols_here), f32)] * shard_count,
        [spec(SMEM), spec(SMEM)] + [spec()] * 4,
        [
            pltpu.VMEM((groups, pairs, cols_here, size * LANES), bf16),
            pltpu.VMEM((local_heads, cols_here, cols_here), f32),
        ],
        flops=4 * rows_here * cols_here * width * local_width,
    )(place, row_mask, alignment, gain, w_query, w_key)
    normed, query, own_shards = own[0], own[1], own[2:]

    def exchange(shards):
        sent = range(1, len(shards))
        return [shards[0]] + [from_behind(shards[k], "depth", k) for k in sent]

    own_shards = exchange(own_shards)

    def project(rows):
        return call(
            functools.partial(value_kernel, cols=cols_here),
            shape((rows.shape[0], pairs, cols_here, size * LANES), bf16),
            [spec()] * 2,
            flops=2 * rows.size * local_width,
        )(rows, w_value)

    values = project(normed)
    tiles, remote_values = [own_shards], []
    for offset in range(1, blocks):
        before = []
        for c in range(CHUNKS):
            last = c + 1 == CHUNKS
            outs = [shape((cores, size * cols_here, width), bf16)]
            if last:
                outs += [shape((shard_rows, cols_here), f32)] * shard_count
                scratch = [pltpu.VMEM((local_heads, cols_here, cols_here), f32)]
            else:
                outs += [shape((pairs, 2 * cols_here, cols_here), f32)]
                scratch = []
            result = call(
                functools.partial(
                    remote_kernel,
                    cores=cores,
                    chunks=CHUNKS,
                    chunk=c,
                    first=c == 0,
                    last=last,
                    shard_cols=shard_cols,
                    shard_count=shard_count,
                ),
                outs,
                [spec(SMEM)] + [spec()] * (cores + 3 + len(before)),
                scratch,
                flops=2 * cores * size * cols_here * width * local_width,
            )(place, *arrived[offset, c], gain, w_key, query, *before)
            if last:
                tiles.append(exchange(result[1:]))
            else:
                before = [result[1]]
            remote_values.append(project(result[0]))

    if direct:
        probs = call(
            functools.partial(
                soft_kernel, tiles=blocks, shard_count=shard_count, head_width=head_width
            ),
            shape((shard_rows, blocks * cols_here), bf16),
            [spec()] * (1 + blocks * shard_count),
            flops=1000000,
        )(valid, *[piece for tile in tiles for piece in tile])
        shards = [probs] + [from_behind(probs, "depth", k) for k in range(1, shard_count)]
    else:
        count = lax.psum(jnp.sum(row_mask.astype(f32)), "depth")
        logits = jnp.concatenate(
            [tile[0][:shard_rows].reshape(local_heads, cols_here, cols_here) for tile in tiles], axis=2
        )
        part = lax.psum_scatter(logits, "depth", scatter_dimension=1, tiled=True)
        mask = valid[None] > 0.5
        scaled = jnp.where(mask, part * lax.rsqrt(f32(head_width) * count), -1e30)
        expo = jnp.where(mask, jnp.exp(scaled - jnp.max(scaled, axis=-1, keepdims=True)), 0.0)
        probs = (expo / jnp.sum(expo, axis=-1, keepdims=True)).astype(bf16)
        probs = lax.all_gather(probs, "depth", axis=1, tiled=True)
        shards = [probs.reshape(shard_rows, blocks * cols_here)]

    heads_out = call(
        functools.partial(
            mix_kernel,
            shard_count=shard_count,
            offsets=blocks - 1,
            cores=cores,
            chunks=CHUNKS,
        ),
        shape((rows_here, cols_here, local_width), bf16),
        [spec(SMEM)] + [spec()] * (shard_count + 1 + len(remote_values)),
        [pltpu.VMEM((pairs, 2 * cols_here, blocks * cols_here), bf16)],
        flops=4 * rows_here * cols_here * blocks * cols_here * local_width,
    )(place, *shards, values, *remote_values)
    parts = [heads_out] + [from_behind(heads_out, "heads", k) for k in range(1, cores)]
    return call(
        functools.partial(out_kernel, cores=cores),
        shape((rows_here, cols_here, local_width), bf16),
        [spec(SMEM), spec(SMEM)] + [spec()] * (cores + 1),
        flops=2 * rows_here * cols_here * width * local_width,
        out_block=(size, cols_here, local_width),
    )(place, row_mask, *parts, w_out)


def solution(mesh):
    in_specs = (
        P(("groups", "depth"), "cols", None),
        P(),
        P(None, "heads"),
        P(None, "heads"),
        P(None, "heads"),
        P(None, "heads"),
        P(("groups", "depth")),
        P(("groups", "cols")),
    )
    out_specs = P(("groups", "depth"), "cols", "heads")

    return jax.shard_map(
        on_device, mesh=mesh, in_specs=in_specs, out_specs=out_specs, check_vma=False
    )
```

```python
import functools

import jax
import jax.numpy as jnp
from jax import lax
from jax.experimental import pallas as pl
from jax.experimental.pallas import tpu as pltpu
from jax.sharding import PartitionSpec as P

HEADS = 12
LANES = 128
CHUNKS = 2
SIZE = 2
LIMIT = 16 << 20
LOWEST = -1e30
PAD = 16


VMEM = pltpu.VMEM
SMEM = pltpu.SMEM
HBM = pltpu.HBM
BF16 = jnp.bfloat16
F32 = jnp.float32


def from_behind(value, axis, steps):
    count = lax.axis_size(axis)
    return lax.ppermute(value, axis, [(s, (s + steps) % count) for s in range(count)])


def spec(space=VMEM):
    return pl.BlockSpec(memory_space=space)


def call(kernel, out_shape, in_specs, scratch=(), flops=0, space=VMEM):
    single = not isinstance(out_shape, (list, tuple))
    shapes = [out_shape] if single else list(out_shape)
    nbytes = sum(s.size * s.dtype.itemsize for s in shapes)
    shapes = [space(s.shape, s.dtype) for s in shapes]
    fn = pl.pallas_call(
        kernel,
        out_shape=shapes,
        in_specs=in_specs,
        out_specs=[spec(space) for _ in shapes],
        scratch_shapes=list(scratch),
        compiler_params=pltpu.CompilerParams(vmem_limit_bytes=LIMIT),
        cost_estimate=pl.CostEstimate(flops=flops, transcendentals=0, bytes_accessed=2 * nbytes),
    )

    def run(*args):
        args = [
            arg
            if block.memory_space == SMEM
            else pltpu.with_memory_space_constraint(arg, block.memory_space)
            for arg, block in zip(args, in_specs, strict=True)
        ]
        out = fn(*args)
        return out[0] if single else out

    return run


def dot(left, right):
    return jnp.dot(left, right, preferred_element_type=F32)


def dot_t(left, right):
    return lax.dot_general(left, right, (((1,), (1,)), ((), ())), preferred_element_type=F32)


def normed_rows(rows, gain):
    values_f = rows.astype(F32)
    average = jnp.mean(values_f, axis=-1, keepdims=True)
    centred = values_f - average
    spread = jnp.mean(centred * centred, axis=-1, keepdims=True)
    return (centred * lax.rsqrt(spread + 1e-05) * gain).astype(BF16)


def load_kernel(place, valid, rows_in, resident, *rest, part_cols):
    last, sems = rest
    part_rows = (last.shape[0] - PAD) // part_cols
    cols = rows_in.shape[1]
    begin = place[1] * part_rows
    copies = [
        pltpu.make_async_copy(
            rows_in.at[begin + r, pl.ds(cols - part_cols, part_cols), :],
            last.at[pl.ds(r * part_cols, part_cols)],
            sems.at[r],
        )
        for r in range(part_rows)
    ]
    copies.append(pltpu.make_async_copy(rows_in, resident, sems.at[part_rows]))
    for copy in copies:
        copy.start()
    tail = last.shape[0] - PAD
    last[tail:, :] = jnp.zeros((PAD, last.shape[1]), BF16)
    last[tail:, 0:cols] = jnp.broadcast_to(valid[...].astype(F32), (PAD, cols)).astype(BF16)
    for copy in copies:
        copy.wait()


def side_by_side(block, first, cols, pair):
    at = slice(pair * LANES, (pair + 1) * LANES)
    pieces = [block[(first + r) * cols : (first + r + 1) * cols, at] for r in range(SIZE)]
    return jnp.concatenate(pieces, axis=1)


def write_shards(total, shards, depth_index):
    slots, cols, _ = total.shape
    count = len(shards)
    part = cols // count
    for k, shard in enumerate(shards):
        begin = pl.multiple_of(lax.bitwise_xor(depth_index, k) * part, part)
        for slot in range(slots):
            rows = total[slot, pl.ds(begin, part), :]
            shard[slot * part : (slot + 1) * part, :] = rows


def own_kernel(place, live, rows_in, gain, w_query, w_key, *rest, shards):
    normed_out, query_out = rest[0], rest[1]
    outs = rest[2 : 2 + shards]
    keys, total = rest[2 + shards :]
    groups, pairs = query_out.shape[0], query_out.shape[1]
    _, cols, width = rows_in.shape
    low = lax.broadcasted_iota(jnp.int32, (cols, LANES), 1) < LANES // 2
    zero = jnp.zeros((cols, LANES), BF16)
    for g in range(groups):
        rows = rows_in[g * SIZE : (g + 1) * SIZE].reshape(SIZE * cols, width)
        normed = normed_rows(rows, gain[...])
        normed_out[g] = normed
        query = dot(normed, w_query[...])
        key = dot(normed, w_key[...]).astype(BF16)
        for r in range(SIZE):
            scale = live[g * SIZE + r].astype(F32)
            piece = (query[r * cols : (r + 1) * cols] * scale).astype(BF16)
            for p in range(pairs):
                both = piece[:, p * LANES : (p + 1) * LANES]
                at = slice(r * LANES, (r + 1) * LANES)
                query_out[g, p, 0:cols, at] = jnp.where(low, both, zero)
                query_out[g, p, cols : 2 * cols, at] = jnp.where(low, zero, both)
        for p in range(pairs):
            keys[g, p] = side_by_side(key, 0, cols, p)
    for p in range(pairs):
        score = dot_t(query_out[0, p], keys[0, p])
        for g in range(1, groups):
            score = score + dot_t(query_out[g, p], keys[g, p])
        total[2 * p] = score[:cols]
        total[2 * p + 1] = score[cols:]
    write_shards(total, outs, place[0])
    real = F32(0)
    for r in range(groups * SIZE):
        real = real + live[r].astype(F32)
    for out in outs:
        out[out.shape[0] - 8 :, :] = jnp.full((8, LANES), real, F32)


def value_kernel(*refs, parts, cols):
    normed, w_value, values = refs[:parts], refs[parts], refs[parts + 1]
    inner, pairs = values.shape[1], values.shape[2]
    for k in range(parts):
        value = dot(normed[k][...], w_value[...]).astype(BF16)
        for g in range(inner):
            for p in range(pairs):
                values[k, g, p] = side_by_side(value, g * SIZE, cols, p)


def own_value_kernel(normed, w_value, values, *, cols):
    for g in range(values.shape[0]):
        value = dot(normed[g], w_value[...]).astype(BF16)
        for p in range(values.shape[1]):
            values[g, p] = side_by_side(value, 0, cols, p)


def remote_kernel(place, part, gain, w_key, query, *rest, step, chunk, part_cols, cores, shards):
    if step > 0:
        before, rest = rest[0], rest[1:]
    normed_out, rest = rest[0], rest[1:]
    last = step + 1 == cores
    used = normed_out.shape[0]
    rows, cols = used // part_cols, part_cols
    pairs, full = query.shape[1], query.shape[2] // 2
    normed = normed_rows(part[0:used, :], gain[...])
    normed_out[...] = normed
    key = dot(normed, w_key[...]).astype(BF16)
    total = rest[shards] if last else rest[0]
    source = lax.rem(place[1] + cores - step, cores)
    inner = rows // SIZE
    low = lax.broadcasted_iota(jnp.int32, (full, LANES), 1) < LANES // 2
    for p in range(pairs):
        score = before[p] if step > 0 else None
        whole = None
        for g in range(inner):
            one = side_by_side(key, g * SIZE, cols, p)
            twice = jnp.concatenate([one, one], axis=0)
            extra = dot_t(query[source * inner + g, p], twice)
            whole = extra if whole is None else whole + extra
        left, right = whole[:full], whole[full:]
        if chunk % 2 == 1:
            left, right = right, left
        packed = jnp.where(low, left, right)
        total[p] = packed if score is None else score + packed
    if last:
        write_shards(total, rest[:shards], place[0])


def added(pieces):
    total = pieces[0][...]
    for piece in pieces[1:]:
        total = total + piece[...]
    return total


def soft_kernel(*rest, shards, offsets, heads, head_width):
    valid, rest = rest[: 1 + offsets], rest[1 + offsets :]
    probs = rest[-1]
    tiles = 1 + offsets * CHUNKS
    sums = [added(rest[t * shards : (t + 1) * shards]) for t in range(tiles)]
    part = probs.shape[0] // heads
    factor = lax.rsqrt(F32(head_width) * sums[0][heads * part : heads * part + 1, 0:1])
    low = lax.broadcasted_iota(jnp.int32, (part, LANES), 1) < LANES // 2
    blocks = 1 + offsets
    masks = [
        jnp.broadcast_to(valid[b][...] > 0.5, (part, LANES)) for b in range(blocks)
    ]
    for h in range(heads):
        pieces = [sums[0][h * part : (h + 1) * part]]
        at = slice(h // 2 * part, (h // 2 + 1) * part)
        for o in range(offsets):
            first, second = sums[1 + o * CHUNKS][at], sums[2 + o * CHUNKS][at]
            if h % 2 == 0:
                pieces.append(jnp.where(low, first, second))
            else:
                pieces.append(pltpu.roll(jnp.where(low, second, first), LANES // 2, 1))
        scaled = [jnp.where(masks[b], pieces[b] * factor, LOWEST) for b in range(blocks)]
        top = jnp.max(functools.reduce(jnp.maximum, scaled), axis=-1, keepdims=True)
        expo = [jnp.where(masks[b], jnp.exp(scaled[b] - top), 0.0) for b in range(blocks)]
        whole = jnp.sum(functools.reduce(jnp.add, expo), axis=-1, keepdims=True)
        for b in range(blocks):
            probs[h * part : (h + 1) * part, b * LANES : (b + 1) * LANES] = (
                expo[b] / whole
            ).astype(BF16)


def mix_kernel(place, *rest, shards, side, cores, offsets):
    own = rest[shards]
    remote = rest[shards + 1 : shards + 1 + offsets * CHUNKS]
    out, probs = rest[shards + 1 + offsets * CHUNKS :]
    _, pairs, cols, lanes = own.shape
    inner = out.shape[0] // SIZE
    part = cols // shards
    for k in range(shards):
        begin = lax.bitwise_xor(place[0], k) * part
        for head in range(2 * pairs):
            at = pl.multiple_of(head % 2 * cols + begin, part)
            probs[head // 2, pl.ds(at, part), :] = rest[k][head * part : (head + 1) * part, :]
    lane = lax.broadcasted_iota(jnp.int32, (cols, lanes), 1)
    low = lax.rem(lane, LANES) < LANES // 2
    step = lax.rem(place[1] + cores - side, cores)
    for g in range(inner):
        for p in range(pairs):
            blocks = [own[side * inner + g, p]]
            blocks += [block[step, g, p] for block in remote]
            mixed = dot(probs[p], jnp.concatenate(blocks, axis=0))
            picked = jnp.where(low, mixed[:cols], mixed[cols:]).astype(BF16)
            for r in range(SIZE):
                out[g * SIZE + r, :, p * LANES : (p + 1) * LANES] = picked[
                    :, r * LANES : (r + 1) * LANES
                ]


def order_kernel(place, w_out, ordered, *, cores):
    local = w_out.shape[0] // cores
    for k in range(cores):
        source = lax.rem(place[1] + cores - k, cores)
        rows = w_out[pl.ds(pl.multiple_of(source * local, local), local), :]
        ordered[k * local : (k + 1) * local, :] = rows


def projected(live, parts, weights, begin, first):
    cols, local = parts[0].shape[1], parts[0].shape[2]
    blocks = [part[begin : begin + SIZE].reshape(SIZE * cols, local) for part in parts]
    total = dot(jnp.concatenate(blocks, axis=1), weights[...])
    results = []
    for r in range(SIZE):
        scale = live[first + begin + r].astype(F32)
        results.append((total[r * cols : (r + 1) * cols] * scale).astype(BF16))
    return results


def project_kernel(live, *rest, cores, first):
    parts, weights, out = rest[:cores], rest[cores], rest[cores + 1]
    for begin in range(0, out.shape[0], SIZE):
        for r, rows in enumerate(projected(live, parts, weights, begin, first)):
            out[begin + r] = rows


def finish_kernel(live, *rest, cores):
    parts, weights = rest[:cores], rest[cores]
    ready = rest[cores + 1 : 2 * cores]
    out, buffer, sems = rest[2 * cores :]
    rows = buffer.shape[0]
    copies = []
    for side, done in enumerate(ready):
        copies.append(
            pltpu.make_async_copy(done, out.at[pl.ds(side * rows, rows)], sems.at[len(copies)])
        )
        copies[-1].start()
    first = (cores - 1) * rows
    for begin in range(0, rows, SIZE):
        for r, block in enumerate(projected(live, parts, weights, begin, first)):
            buffer[begin + r] = block
        copies.append(
            pltpu.make_async_copy(
                buffer.at[pl.ds(begin, SIZE)],
                out.at[pl.ds(first + begin, SIZE)],
                sems.at[len(copies)],
            )
        )
        copies[-1].start()
    for copy in copies:
        copy.wait()


def on_device(alignment, norm_gain, w_query, w_key, w_value, w_out, row_mask, col_valid):
    rows_here, cols_here, width = alignment.shape
    local_width = w_query.shape[1]
    head_width = width // HEADS
    local_heads = local_width // head_width
    pairs = local_heads // 2
    offsets = lax.axis_size("cols") - 1
    depth = lax.axis_size("depth")
    cores = lax.axis_size("heads")
    core = lax.axis_index("heads")
    place = jnp.stack([lax.axis_index("depth"), core]).astype(jnp.int32)
    part_rows = rows_here // cores
    inner = part_rows // SIZE
    groups = rows_here // SIZE
    part_cols = cols_here // CHUNKS
    direct = depth in (2, 4, 8) and cols_here % (16 * depth) == 0
    shards = depth if direct else 1
    part = cols_here // shards
    lanes = SIZE * LANES
    total_cols = (1 + offsets) * cols_here
    shape = jax.ShapeDtypeStruct
    gain = norm_gain[None, :]

    first = lax.dynamic_slice(
        alignment, (core * part_rows, 0, 0), (part_rows, cols_here - part_cols, width)
    )
    sent = [
        first[:, c * part_cols : (c + 1) * part_cols].reshape(part_rows * part_cols, width)
        for c in range(CHUNKS - 1)
    ]
    resident, last_chunk = call(
        functools.partial(load_kernel, part_cols=part_cols),
        [
            shape((rows_here, cols_here, width), BF16),
            shape((part_rows * part_cols + PAD, width), BF16),
        ],
        [spec(SMEM), spec(), spec(HBM)],
        [pltpu.SemaphoreType.DMA((part_rows + 1,))],
    )(place, col_valid[None, :], alignment)
    sent.append(last_chunk)
    arrived = {}
    for offset in range(1, offsets + 1):
        for c in range(CHUNKS):
            mine = from_behind(sent[c], "cols", offset)
            arrived[offset, c] = [mine] + [from_behind(mine, "heads", k) for k in range(1, cores)]

    def exchange(values):
        received = [values[0]]
        for k in range(1, shards):
            swapped = [(source, source ^ k) for source in range(depth)]
            received.append(lax.ppermute(values[k], "depth", swapped))
        return received

    own = call(
        functools.partial(own_kernel, shards=shards),
        [
            shape((groups, SIZE * cols_here, width), BF16),
            shape((groups, pairs, 2 * cols_here, lanes), BF16),
        ]
        + [shape((local_heads * part + 8, cols_here), F32)] * shards,
        [spec(SMEM), spec(SMEM)] + [spec()] * 4,
        [
            pltpu.VMEM((groups, pairs, cols_here, lanes), BF16),
            pltpu.VMEM((local_heads, cols_here, cols_here), F32),
        ],
        flops=4 * rows_here * cols_here * width * local_width,
    )(place, row_mask, resident, gain, w_query, w_key)
    normed, query, own_sums = own[0], own[1], exchange(own[2:])

    own_values = call(
        functools.partial(own_value_kernel, cols=cols_here),
        shape((groups, pairs, cols_here, lanes), BF16),
        [spec()] * 2,
        flops=2 * rows_here * cols_here * width * local_width,
    )(normed, w_value)
    ordered = call(
        functools.partial(order_kernel, cores=cores), shape(w_out.shape, BF16), [spec(SMEM), spec()]
    )(place, w_out)

    tiles, remote_values = [], []
    for offset in range(1, offsets + 1):
        for c in range(CHUNKS):
            before, rows_of = [], []
            for k in range(cores):
                outs = [shape((part_rows * part_cols, width), BF16)]
                scratch = []
                if k + 1 == cores:
                    outs += [shape((pairs * part, LANES), F32)] * shards
                    scratch = [pltpu.VMEM((pairs, cols_here, LANES), F32)]
                else:
                    outs += [shape((pairs, cols_here, LANES), F32)]
                result = call(
                    functools.partial(
                        remote_kernel,
                        step=k,
                        chunk=c,
                        part_cols=part_cols,
                        cores=cores,
                        shards=shards,
                    ),
                    outs,
                    [spec(SMEM)] + [spec()] * (4 + len(before)),
                    scratch,
                    flops=2 * part_rows * part_cols * width * local_width,
                )(place, arrived[offset, c][k], gain, w_key, query, *before)
                rows_of.append(result[0])
                before = [result[1]]
            tiles.append(exchange(result[1:]))
            remote_values.append(
                call(
                    functools.partial(value_kernel, parts=cores, cols=part_cols),
                    shape((cores, inner, pairs, part_cols, lanes), BF16),
                    [spec()] * (cores + 1),
                    flops=2 * cores * part_rows * part_cols * width * local_width,
                )(*rows_of, w_value)
            )

    valid_tiles = [col_valid.astype(BF16)[None, :]]
    for offset in range(1, offsets + 1):
        valid_tiles.append(arrived[offset, CHUNKS - 1][0][-PAD : 1 - PAD, :cols_here])
    if direct:
        valid = [tile.astype(F32) for tile in valid_tiles]
        probs = call(
            functools.partial(
                soft_kernel,
                shards=shards,
                offsets=offsets,
                heads=local_heads,
                head_width=head_width,
            ),
            shape((local_heads * part, total_cols), BF16),
            [spec()] * (1 + offsets + shards * (1 + len(tiles))),
            flops=1000000,
        )(*valid, *own_sums, *[piece for tile in tiles for piece in tile])
        probs = exchange([probs] * shards)
    else:
        count = lax.psum(jnp.sum(row_mask.astype(F32)), "depth")
        own_part = own_sums[0][: local_heads * cols_here]
        blocks = [own_part.reshape(local_heads, cols_here, cols_here)]
        for index, tile in enumerate(tiles):
            packed = tile[0].reshape(pairs, cols_here, 2, part_cols)
            packed = packed[:, :, ::-1] if index % CHUNKS % 2 == 1 else packed
            packed = jnp.transpose(packed, (0, 2, 1, 3))
            blocks.append(packed.reshape(local_heads, cols_here, part_cols))
        logits = jnp.concatenate(blocks, axis=2)
        share = lax.psum_scatter(logits, "depth", scatter_dimension=1, tiled=True)
        mask = jnp.concatenate(valid_tiles, axis=1)[None] > 0.5
        scaled = jnp.where(mask, share * lax.rsqrt(F32(head_width) * count), LOWEST)
        expo = jnp.where(mask, jnp.exp(scaled - jnp.max(scaled, axis=-1, keepdims=True)), 0.0)
        probs = (expo / jnp.sum(expo, axis=-1, keepdims=True)).astype(BF16)
        probs = lax.all_gather(probs, "depth", axis=1, tiled=True)
        probs = [probs.reshape(local_heads * cols_here, total_cols)]

    finished = []
    for side in range(cores):
        mine = call(
            functools.partial(
                mix_kernel, shards=shards, side=side, cores=cores, offsets=offsets
            ),
            shape((part_rows, cols_here, local_width), BF16),
            [spec(SMEM)] + [spec()] * (shards + 1 + len(remote_values)),
            [pltpu.VMEM((pairs, 2 * cols_here, total_cols), BF16)],
            flops=4 * part_rows * cols_here * total_cols * local_width,
        )(place, *probs, own_values, *remote_values)
        parts = [mine] + [from_behind(mine, "heads", k) for k in range(1, cores)]
        if side + 1 < cores:
            finished.append(
                call(
                    functools.partial(project_kernel, cores=cores, first=side * part_rows),
                    shape((part_rows, cols_here, local_width), BF16),
                    [spec(SMEM)] + [spec()] * (cores + 1),
                    flops=2 * part_rows * cols_here * width * local_width,
                )(row_mask, *parts, ordered)
            )
    return call(
        functools.partial(finish_kernel, cores=cores),
        shape((rows_here, cols_here, local_width), BF16),
        [spec(SMEM)] + [spec()] * (2 * cores),
        [
            pltpu.VMEM((part_rows, cols_here, local_width), BF16),
            pltpu.SemaphoreType.DMA((cores - 1 + inner,)),
        ],
        flops=2 * part_rows * cols_here * width * local_width,
        space=HBM,
    )(row_mask, *parts, ordered, *finished)


def solution(mesh):
    in_specs = (
        P(("groups", "depth"), "cols", None),
        P(),
        P(None, "heads"),
        P(None, "heads"),
        P(None, "heads"),
        P(None, "heads"),
        P(("groups", "depth")),
        P(("groups", "cols")),
    )
    out_specs = P(("groups", "depth"), "cols", "heads")

    return jax.shard_map(
        on_device, mesh=mesh, in_specs=in_specs, out_specs=out_specs, check_vma=False
    )
```

```python
import functools

import jax
import jax.numpy as jnp
from jax import lax
from jax.experimental import pallas as pl
from jax.experimental.pallas import tpu as pltpu
from jax.sharding import PartitionSpec as P

HEADS = 12
LANES = 128
CHUNKS = 2
SIZE = 2
LIMIT = 16 << 20
LOWEST = -1e30
PAD = 16


VMEM = pltpu.VMEM
SMEM = pltpu.SMEM
HBM = pltpu.HBM
BF16 = jnp.bfloat16
F32 = jnp.float32


def from_behind(value, axis, steps):
    count = lax.axis_size(axis)
    return lax.ppermute(value, axis, [(s, (s + steps) % count) for s in range(count)])


def spec(space=VMEM):
    return pl.BlockSpec(memory_space=space)


def call(kernel, out_shape, in_specs, scratch=(), flops=0, space=VMEM):
    single = not isinstance(out_shape, (list, tuple))
    shapes = [out_shape] if single else list(out_shape)
    nbytes = sum(s.size * s.dtype.itemsize for s in shapes)
    shapes = [space(s.shape, s.dtype) for s in shapes]
    fn = pl.pallas_call(
        kernel,
        out_shape=shapes,
        in_specs=in_specs,
        out_specs=[spec(space) for _ in shapes],
        scratch_shapes=list(scratch),
        compiler_params=pltpu.CompilerParams(vmem_limit_bytes=LIMIT),
        cost_estimate=pl.CostEstimate(flops=flops, transcendentals=0, bytes_accessed=2 * nbytes),
    )

    def run(*args):
        args = [
            arg
            if block.memory_space == SMEM
            else pltpu.with_memory_space_constraint(arg, block.memory_space)
            for arg, block in zip(args, in_specs, strict=True)
        ]
        out = fn(*args)
        return out[0] if single else out

    return run


def dot(left, right):
    return jnp.dot(left, right, preferred_element_type=F32)


def dot_t(left, right):
    return lax.dot_general(left, right, (((1,), (1,)), ((), ())), preferred_element_type=F32)


def normed_rows(rows, gain):
    values_f = rows.astype(F32)
    average = jnp.mean(values_f, axis=-1, keepdims=True)
    centred = values_f - average
    spread = jnp.mean(centred * centred, axis=-1, keepdims=True)
    return (centred * lax.rsqrt(spread + 1e-05) * gain).astype(BF16)


def load_kernel(place, valid, rows_in, resident, last, flags, sems, *, part_cols):
    part_rows = (last.shape[0] - PAD) // part_cols
    rows_here, cols, _ = resident.shape
    begin = place[1] * part_rows
    first = pltpu.make_async_copy(valid, flags, sems.at[part_rows + rows_here])
    first.start()
    copies = [
        pltpu.make_async_copy(
            rows_in.at[begin + r, pl.ds(cols - part_cols, part_cols), :],
            last.at[pl.ds(r * part_cols, part_cols)],
            sems.at[r],
        )
        for r in range(part_rows)
    ]
    for r in range(rows_here):
        sem = sems.at[part_rows + r]
        copies.append(pltpu.make_async_copy(rows_in.at[r], resident.at[r], sem))
    for copy in copies:
        copy.start()
    first.wait()
    tail = last.shape[0] - PAD
    last[tail:, :] = jnp.zeros((PAD, last.shape[1]), BF16)
    last[tail:, 0:cols] = jnp.broadcast_to(flags[...].astype(F32), (PAD, cols)).astype(BF16)
    for copy in copies:
        copy.wait()


def side_by_side(block, first, cols, pair):
    at = slice(pair * LANES, (pair + 1) * LANES)
    pieces = [block[(first + r) * cols : (first + r + 1) * cols, at] for r in range(SIZE)]
    return jnp.concatenate(pieces, axis=1)


def write_shards(total, shards, depth_index):
    slots, cols, _ = total.shape
    count = len(shards)
    part = cols // count
    for k, shard in enumerate(shards):
        begin = pl.multiple_of(lax.bitwise_xor(depth_index, k) * part, part)
        for slot in range(slots):
            rows = total[slot, pl.ds(begin, part), :]
            shard[slot * part : (slot + 1) * part, :] = rows


def own_kernel(place, live, rows_in, gain, w_query, w_key, *rest, shards):
    normed_out, query_out = rest[0], rest[1]
    outs = rest[2 : 2 + shards]
    keys, total = rest[2 + shards :]
    groups, pairs = query_out.shape[0], query_out.shape[1]
    _, cols, width = rows_in.shape
    low = lax.broadcasted_iota(jnp.int32, (cols, LANES), 1) < LANES // 2
    zero = jnp.zeros((cols, LANES), BF16)
    local = w_query.shape[1]
    weights = jnp.concatenate([w_query[...], w_key[...]], axis=1)
    for g in range(groups):
        rows = rows_in[g * SIZE : (g + 1) * SIZE].reshape(SIZE * cols, width)
        normed = normed_rows(rows, gain[...])
        normed_out[g] = normed
        both_sides = dot(normed, weights)
        query, key = both_sides[:, :local], both_sides[:, local:].astype(BF16)
        for r in range(SIZE):
            scale = live[g * SIZE + r].astype(F32)
            piece = (query[r * cols : (r + 1) * cols] * scale).astype(BF16)
            for p in range(pairs):
                both = piece[:, p * LANES : (p + 1) * LANES]
                at = slice(r * LANES, (r + 1) * LANES)
                query_out[g, p, 0:cols, at] = jnp.where(low, both, zero)
                query_out[g, p, cols : 2 * cols, at] = jnp.where(low, zero, both)
        for p in range(pairs):
            keys[g, p] = side_by_side(key, 0, cols, p)
    for p in range(pairs):
        score = dot_t(query_out[0, p], keys[0, p])
        for g in range(1, groups):
            score = score + dot_t(query_out[g, p], keys[g, p])
        total[2 * p] = score[:cols]
        total[2 * p + 1] = score[cols:]
    write_shards(total, outs, place[0])
    real = F32(0)
    for r in range(groups * SIZE):
        real = real + live[r].astype(F32)
    for out in outs:
        out[out.shape[0] - 8 :, :] = jnp.full((8, LANES), real, F32)


def value_kernel(*refs, parts, cols):
    normed, w_value, values = refs[:parts], refs[parts], refs[parts + 1]
    inner, pairs = values.shape[1], values.shape[2]
    for k in range(parts):
        value = dot(normed[k][...], w_value[...]).astype(BF16)
        for g in range(inner):
            for p in range(pairs):
                values[k, g, p] = side_by_side(value, g * SIZE, cols, p)


def own_value_kernel(normed, w_value, values, *, cols):
    for g in range(values.shape[0]):
        value = dot(normed[g], w_value[...]).astype(BF16)
        for p in range(values.shape[1]):
            values[g, p] = side_by_side(value, 0, cols, p)


def remote_kernel(place, part, gain, w_key, query, *rest, step, chunk, part_cols, cores, shards):
    if step > 0:
        before, rest = rest[0], rest[1:]
    normed_out, rest = rest[0], rest[1:]
    last = step + 1 == cores
    used = normed_out.shape[0]
    rows, cols = used // part_cols, part_cols
    pairs, full = query.shape[1], query.shape[2] // 2
    normed = normed_rows(part[0:used, :], gain[...])
    normed_out[...] = normed
    key = dot(normed, w_key[...]).astype(BF16)
    total = rest[shards] if last else rest[0]
    source = lax.rem(place[1] + cores - step, cores)
    inner = rows // SIZE
    low = lax.broadcasted_iota(jnp.int32, (full, LANES), 1) < LANES // 2
    for p in range(pairs):
        score = before[p] if step > 0 else None
        whole = None
        for g in range(inner):
            one = side_by_side(key, g * SIZE, cols, p)
            twice = jnp.concatenate([one, one], axis=0)
            extra = dot_t(query[source * inner + g, p], twice)
            whole = extra if whole is None else whole + extra
        left, right = whole[:full], whole[full:]
        if chunk % 2 == 1:
            left, right = right, left
        packed = jnp.where(low, left, right)
        total[p] = packed if score is None else score + packed
    if last:
        write_shards(total, rest[:shards], place[0])


def added(pieces):
    total = pieces[0][...]
    for piece in pieces[1:]:
        total = total + piece[...]
    return total


def own_soft_kernel(valid, *rest, heads, head_width):
    pieces, probs, stats = rest[:-2], rest[-2], rest[-1]
    total = added(pieces)
    rows = probs.shape[0]
    factor = lax.rsqrt(F32(head_width) * total[rows : rows + 1, 0:1])
    mask = jnp.broadcast_to(valid[...] > 0.5, (rows, LANES))
    scaled = jnp.where(mask, total[:rows] * factor, LOWEST)
    top = jnp.max(scaled, axis=-1, keepdims=True)
    expo = jnp.where(mask, jnp.exp(scaled - top), 0.0)
    whole = jnp.sum(expo, axis=-1, keepdims=True)
    probs[...] = expo.astype(BF16)
    stats[0] = jnp.broadcast_to(top, (rows, LANES))
    stats[1] = jnp.broadcast_to(whole, (rows, LANES))
    stats[2] = jnp.broadcast_to(factor, (rows, LANES))


def diagonal(rows):
    row = lax.broadcasted_iota(jnp.int32, (rows, LANES), 0)
    return row == lax.broadcasted_iota(jnp.int32, (rows, LANES), 1)


def last_soft_kernel(*rest, shards, offsets, heads):
    valid, stats, probs = rest[:offsets], rest[offsets], rest[-1]
    rest = rest[offsets + 1 : -1]
    sums = [added(rest[t * shards : (t + 1) * shards]) for t in range(offsets * CHUNKS)]
    rows = stats.shape[1]
    part = rows // heads
    low = lax.broadcasted_iota(jnp.int32, (part, LANES), 1) < LANES // 2
    old, own, factor = stats[0], stats[1], stats[2]
    masks, scaled = [], []
    for o in range(offsets):
        pieces = []
        for h in range(heads):
            at = slice(h // 2 * part, (h // 2 + 1) * part)
            first, second = sums[o * CHUNKS][at], sums[o * CHUNKS + 1][at]
            if h % 2 == 0:
                pieces.append(jnp.where(low, first, second))
            else:
                pieces.append(pltpu.roll(jnp.where(low, second, first), LANES // 2, 1))
        masks.append(jnp.broadcast_to(valid[o][...] > 0.5, (rows, LANES)))
        piece = jnp.concatenate(pieces, axis=0)
        scaled.append(jnp.where(masks[o], piece * factor, LOWEST))
    highest = jnp.max(functools.reduce(jnp.maximum, scaled), axis=-1, keepdims=True)
    top = jnp.maximum(old, highest)
    expo = [jnp.where(masks[o], jnp.exp(scaled[o] - top), 0.0) for o in range(offsets)]
    extra = jnp.sum(functools.reduce(jnp.add, expo), axis=-1, keepdims=True)
    shift = jnp.exp(old - top)
    whole = shift * own + extra
    for o in range(offsets):
        probs[0:rows, o * LANES : (o + 1) * LANES] = (expo[o] / whole).astype(BF16)
    scale = shift / whole
    kept = diagonal(part)
    lines = []
    for h in range(heads):
        block = jnp.where(kept, scale[h * part : (h + 1) * part], 0.0)
        lines.append(jnp.sum(block, axis=0, keepdims=True))
    lines = jnp.concatenate(lines + [jnp.zeros((8 - heads, LANES), F32)], axis=0)
    coarse = lines.astype(BF16).astype(F32)
    tail = jnp.concatenate([coarse, lines - coarse], axis=0)
    probs[rows:, 0:LANES] = tail.astype(BF16)


def collect(place, owns, others, probs, heads):
    rows = owns[0].shape[0]
    part = rows // heads
    cols = probs.shape[1] // 2
    kept = diagonal(part)
    for k in range(len(owns)):
        begin = lax.bitwise_xor(place[0], k) * part
        tail = others[k][rows:, 0:LANES].astype(F32)
        lines = tail[0:8] + tail[8:16]
        for head in range(heads):
            at = pl.ds(pl.multiple_of(head % 2 * cols + begin, part), part)
            mine = slice(head * part, (head + 1) * part)
            line = jnp.where(kept, jnp.broadcast_to(lines[head : head + 1], (part, LANES)), 0.0)
            scale = jnp.sum(line, axis=-1, keepdims=True)
            own = owns[k][mine, :].astype(F32) * scale
            probs[head // 2, at, 0:LANES] = own.astype(BF16)
            probs[head // 2, at, LANES:] = others[k][mine, :]


def mix_kernel(place, *rest, side, cores, tiles, shards, heads):
    if shards:
        rest, probs = rest[:-1], rest[-1]
        collect(place, rest[:shards], rest[shards : 2 * shards], probs, heads)
        rest = rest[2 * shards :]
    else:
        probs, rest = rest[0], rest[1:]
    own, remote, out = rest[0], rest[1 : 1 + tiles], rest[1 + tiles]
    _, pairs, cols, lanes = own.shape
    inner = out.shape[0] // SIZE
    lane = lax.broadcasted_iota(jnp.int32, (cols, lanes), 1)
    low = lax.rem(lane, LANES) < LANES // 2
    step = lax.rem(place[1] + cores - side, cores)
    for g in range(inner):
        for p in range(pairs):
            blocks = [own[side * inner + g, p]]
            blocks += [block[step, g, p] for block in remote]
            mixed = dot(probs[p], jnp.concatenate(blocks, axis=0))
            picked = jnp.where(low, mixed[:cols], mixed[cols:]).astype(BF16)
            for r in range(SIZE):
                out[g * SIZE + r, :, p * LANES : (p + 1) * LANES] = picked[
                    :, r * LANES : (r + 1) * LANES
                ]


def order_kernel(place, w_out, ordered, *, cores):
    local = w_out.shape[0] // cores
    for k in range(cores):
        source = lax.rem(place[1] + cores - k, cores)
        rows = w_out[pl.ds(pl.multiple_of(source * local, local), local), :]
        ordered[k * local : (k + 1) * local, :] = rows


def projected(live, parts, weights, begin, first):
    cols, local = parts[0].shape[1], parts[0].shape[2]
    blocks = [part[begin : begin + SIZE].reshape(SIZE * cols, local) for part in parts]
    total = dot(jnp.concatenate(blocks, axis=1), weights[...])
    results = []
    for r in range(SIZE):
        scale = live[first + begin + r].astype(F32)
        results.append((total[r * cols : (r + 1) * cols] * scale).astype(BF16))
    return results


def project_kernel(live, *rest, cores, first):
    parts, weights, out = rest[:cores], rest[cores], rest[cores + 1]
    for begin in range(0, out.shape[0], SIZE):
        for r, rows in enumerate(projected(live, parts, weights, begin, first)):
            out[begin + r] = rows


def finish_kernel(live, *rest, cores):
    parts, weights = rest[:cores], rest[cores]
    ready = rest[cores + 1 : 2 * cores]
    out, buffer, sems = rest[2 * cores :]
    rows = buffer.shape[0]
    copies = []
    for side, done in enumerate(ready):
        copies.append(
            pltpu.make_async_copy(done, out.at[pl.ds(side * rows, rows)], sems.at[len(copies)])
        )
        copies[-1].start()
    first = (cores - 1) * rows
    for begin in range(0, rows, SIZE):
        for r, block in enumerate(projected(live, parts, weights, begin, first)):
            buffer[begin + r] = block
        copies.append(
            pltpu.make_async_copy(
                buffer.at[pl.ds(begin, SIZE)],
                out.at[pl.ds(first + begin, SIZE)],
                sems.at[len(copies)],
            )
        )
        copies[-1].start()
    for copy in copies:
        copy.wait()


def on_device(alignment, norm_gain, w_query, w_key, w_value, w_out, row_mask, col_valid):
    rows_here, cols_here, width = alignment.shape
    local_width = w_query.shape[1]
    head_width = width // HEADS
    local_heads = local_width // head_width
    pairs = local_heads // 2
    offsets = lax.axis_size("cols") - 1
    depth = lax.axis_size("depth")
    cores = lax.axis_size("heads")
    core = lax.axis_index("heads")
    place = jnp.stack([lax.axis_index("depth"), core]).astype(jnp.int32)
    part_rows = rows_here // cores
    inner = part_rows // SIZE
    groups = rows_here // SIZE
    part_cols = cols_here // CHUNKS
    direct = depth in (2, 4, 8) and cols_here % (16 * depth) == 0
    shards = depth if direct else 1
    part = cols_here // shards
    lanes = SIZE * LANES
    total_cols = (1 + offsets) * cols_here
    shape = jax.ShapeDtypeStruct
    gain = norm_gain[None, :]

    first = lax.dynamic_slice(
        alignment, (core * part_rows, 0, 0), (part_rows, cols_here - part_cols, width)
    )
    sent = [first.reshape(part_rows * part_cols, width)]
    resident, last_chunk = call(
        functools.partial(load_kernel, part_cols=part_cols),
        [
            shape((rows_here, cols_here, width), BF16),
            shape((part_rows * part_cols + PAD, width), BF16),
        ],
        [spec(SMEM), spec(HBM), spec(HBM)],
        [
            pltpu.VMEM((1, cols_here), jnp.int32),
            pltpu.SemaphoreType.DMA((part_rows + rows_here + 1,)),
        ],
    )(place, col_valid[None, :], alignment)
    sent.append(last_chunk)
    arrived = {}
    for offset in range(1, offsets + 1):
        for c in range(CHUNKS):
            mine = from_behind(sent[c], "cols", offset)
            arrived[offset, c] = [mine] + [from_behind(mine, "heads", k) for k in range(1, cores)]

    def exchange(values):
        received = [values[0]]
        for k in range(1, shards):
            swapped = [(source, source ^ k) for source in range(depth)]
            received.append(lax.ppermute(values[k], "depth", swapped))
        return received

    own = call(
        functools.partial(own_kernel, shards=shards),
        [
            shape((groups, SIZE * cols_here, width), BF16),
            shape((groups, pairs, 2 * cols_here, lanes), BF16),
        ]
        + [shape((local_heads * part + 8, cols_here), F32)] * shards,
        [spec(SMEM), spec(SMEM)] + [spec()] * 4,
        [
            pltpu.VMEM((groups, pairs, cols_here, lanes), BF16),
            pltpu.VMEM((local_heads, cols_here, cols_here), F32),
        ],
        flops=4 * rows_here * cols_here * width * local_width,
    )(place, row_mask, resident, gain, w_query, w_key)
    normed, query, own_sums = own[0], own[1], exchange(own[2:])

    own_values = call(
        functools.partial(own_value_kernel, cols=cols_here),
        shape((groups, pairs, cols_here, lanes), BF16),
        [spec()] * 2,
        flops=2 * rows_here * cols_here * width * local_width,
    )(normed, w_value)
    ordered = call(
        functools.partial(order_kernel, cores=cores), shape(w_out.shape, BF16), [spec(SMEM), spec()]
    )(place, w_out)

    tiles, remote_values = [], []
    for offset in range(1, offsets + 1):
        for c in range(CHUNKS):
            before, rows_of = [], []
            for k in range(cores):
                outs = [shape((part_rows * part_cols, width), BF16)]
                scratch = []
                if k + 1 == cores:
                    outs += [shape((pairs * part, LANES), F32)] * shards
                    scratch = [pltpu.VMEM((pairs, cols_here, LANES), F32)]
                else:
                    outs += [shape((pairs, cols_here, LANES), F32)]
                result = call(
                    functools.partial(
                        remote_kernel,
                        step=k,
                        chunk=c,
                        part_cols=part_cols,
                        cores=cores,
                        shards=shards,
                    ),
                    outs,
                    [spec(SMEM)] + [spec()] * (4 + len(before)),
                    scratch,
                    flops=2 * part_rows * part_cols * width * local_width,
                )(place, arrived[offset, c][k], gain, w_key, query, *before)
                rows_of.append(result[0])
                before = [result[1]]
            tiles.append(exchange(result[1:]))
            remote_values.append(
                call(
                    functools.partial(value_kernel, parts=cores, cols=part_cols),
                    shape((cores, inner, pairs, part_cols, lanes), BF16),
                    [spec()] * (cores + 1),
                    flops=2 * cores * part_rows * part_cols * width * local_width,
                )(*rows_of, w_value)
            )

    valid_tiles = [col_valid.astype(BF16)[None, :]]
    for offset in range(1, offsets + 1):
        valid_tiles.append(arrived[offset, CHUNKS - 1][0][-PAD : 1 - PAD, :cols_here])
    if direct:
        valid = [tile.astype(F32) for tile in valid_tiles]
        rows = local_heads * part
        own_probs, stats = call(
            functools.partial(own_soft_kernel, heads=local_heads, head_width=head_width),
            [shape((rows, LANES), BF16), shape((3, rows, LANES), F32)],
            [spec()] * (1 + shards),
            flops=1000000,
        )(valid[0], *own_sums)
        own_probs = exchange([own_probs] * shards)
        probs = call(
            functools.partial(
                last_soft_kernel, shards=shards, offsets=offsets, heads=local_heads
            ),
            shape((rows + PAD, offsets * LANES), BF16),
            [spec()] * (1 + offsets + shards * len(tiles)),
            flops=1000000,
        )(*valid[1:], stats, *[piece for tile in tiles for piece in tile])
        probs = exchange([probs] * shards)
        probs = own_probs + probs
    else:
        count = lax.psum(jnp.sum(row_mask.astype(F32)), "depth")
        own_part = own_sums[0][: local_heads * cols_here]
        blocks = [own_part.reshape(local_heads, cols_here, cols_here)]
        for index, tile in enumerate(tiles):
            packed = tile[0].reshape(pairs, cols_here, 2, part_cols)
            packed = packed[:, :, ::-1] if index % CHUNKS % 2 == 1 else packed
            packed = jnp.transpose(packed, (0, 2, 1, 3))
            blocks.append(packed.reshape(local_heads, cols_here, part_cols))
        logits = jnp.concatenate(blocks, axis=2)
        share = lax.psum_scatter(logits, "depth", scatter_dimension=1, tiled=True)
        mask = jnp.concatenate(valid_tiles, axis=1)[None] > 0.5
        scaled = jnp.where(mask, share * lax.rsqrt(F32(head_width) * count), LOWEST)
        expo = jnp.where(mask, jnp.exp(scaled - jnp.max(scaled, axis=-1, keepdims=True)), 0.0)
        probs = (expo / jnp.sum(expo, axis=-1, keepdims=True)).astype(BF16)
        probs = lax.all_gather(probs, "depth", axis=1, tiled=True)
        probs = [probs.reshape(pairs, 2 * cols_here, total_cols)]

    finished = []
    for side in range(cores):
        gathers = len(probs) // 2
        outs = [shape((part_rows, cols_here, local_width), BF16)]
        if gathers:
            outs.append(shape((pairs, 2 * cols_here, total_cols), BF16))
        mixed = call(
            functools.partial(
                mix_kernel,
                side=side,
                cores=cores,
                tiles=len(tiles),
                shards=gathers,
                heads=local_heads,
            ),
            outs,
            [spec(SMEM)] + [spec()] * (len(probs) + 1 + len(remote_values)),
            flops=4 * part_rows * cols_here * total_cols * local_width,
        )(place, *probs, own_values, *remote_values)
        mine, probs = mixed[0], mixed[1:] if gathers else probs
        parts = [mine] + [from_behind(mine, "heads", k) for k in range(1, cores)]
        if side + 1 < cores:
            finished.append(
                call(
                    functools.partial(project_kernel, cores=cores, first=side * part_rows),
                    shape((part_rows, cols_here, local_width), BF16),
                    [spec(SMEM)] + [spec()] * (cores + 1),
                    flops=2 * part_rows * cols_here * width * local_width,
                )(row_mask, *parts, ordered)
            )
    return call(
        functools.partial(finish_kernel, cores=cores),
        shape((rows_here, cols_here, local_width), BF16),
        [spec(SMEM)] + [spec()] * (2 * cores),
        [
            pltpu.VMEM((part_rows, cols_here, local_width), BF16),
            pltpu.SemaphoreType.DMA((cores - 1 + inner,)),
        ],
        flops=2 * part_rows * cols_here * width * local_width,
        space=HBM,
    )(row_mask, *parts, ordered, *finished)


def solution(mesh):
    in_specs = (
        P(("groups", "depth"), "cols", None),
        P(),
        P(None, "heads"),
        P(None, "heads"),
        P(None, "heads"),
        P(None, "heads"),
        P(("groups", "depth")),
        P(("groups", "cols")),
    )
    out_specs = P(("groups", "depth"), "cols", "heads")

    return jax.shard_map(
        on_device, mesh=mesh, in_specs=in_specs, out_specs=out_specs, check_vma=False
    )
```

```python
import functools

import jax
import jax.numpy as jnp
from jax import lax
from jax.experimental import pallas as pl
from jax.experimental.pallas import tpu as pltpu
from jax.sharding import PartitionSpec as P

HEADS = 12
LANES = 128
CHUNKS = 2
SIZE = 2
LIMIT = 16 << 20
LOWEST = -1e30
PAD = 16


VMEM = pltpu.VMEM
SMEM = pltpu.SMEM
HBM = pltpu.HBM
BF16 = jnp.bfloat16
F32 = jnp.float32


def from_behind(value, axis, steps):
    count = lax.axis_size(axis)
    return lax.ppermute(value, axis, [(s, (s + steps) % count) for s in range(count)])


def spec(space=VMEM):
    return pl.BlockSpec(memory_space=space)


def call(kernel, out_shape, in_specs, scratch=(), flops=0, space=VMEM):
    single = not isinstance(out_shape, (list, tuple))
    shapes = [out_shape] if single else list(out_shape)
    nbytes = sum(s.size * s.dtype.itemsize for s in shapes)
    shapes = [space(s.shape, s.dtype) for s in shapes]
    fn = pl.pallas_call(
        kernel,
        out_shape=shapes,
        in_specs=in_specs,
        out_specs=[spec(space) for _ in shapes],
        scratch_shapes=list(scratch),
        compiler_params=pltpu.CompilerParams(vmem_limit_bytes=LIMIT),
        cost_estimate=pl.CostEstimate(flops=flops, transcendentals=0, bytes_accessed=2 * nbytes),
    )

    def run(*args):
        args = [
            arg
            if block.memory_space == SMEM
            else pltpu.with_memory_space_constraint(arg, block.memory_space)
            for arg, block in zip(args, in_specs, strict=True)
        ]
        out = fn(*args)
        return out[0] if single else out

    return run


def dot(left, right):
    return jnp.dot(left, right, preferred_element_type=F32)


def dot_t(left, right):
    return lax.dot_general(left, right, (((1,), (1,)), ((), ())), preferred_element_type=F32)


def normed_rows(rows, gain):
    values_f = rows.astype(F32)
    average = jnp.mean(values_f, axis=-1, keepdims=True)
    centred = values_f - average
    spread = jnp.mean(centred * centred, axis=-1, keepdims=True)
    return (centred * lax.rsqrt(spread + 1e-05) * gain).astype(BF16)


def load_kernel(valid, rows_in, resident, *rest, part_cols):
    lasts, flags, sems = rest[:-2], rest[-2], rest[-1]
    rows_here, cols, _ = resident.shape
    some = lasts[-1].shape[0] // part_cols
    begin = lax.axis_index("heads") * some * len(lasts)
    first = pltpu.make_async_copy(valid, flags, sems.at[rows_here + some * len(lasts)])
    first.start()
    copies = []
    for r in range(some * len(lasts)):
        source = rows_in.at[begin + r, pl.ds(cols - part_cols, part_cols), :]
        target = lasts[r // some].at[pl.ds(r % some * part_cols, part_cols)]
        copies.append(pltpu.make_async_copy(source, target, sems.at[rows_here + r]))
    for r in range(rows_here):
        copies.append(pltpu.make_async_copy(rows_in.at[r], resident.at[r], sems.at[r]))
    for copy in copies:
        copy.start()
    first.wait()
    tail = some * part_cols
    lasts[0][tail:, :] = jnp.zeros((PAD, lasts[0].shape[1]), BF16)
    lasts[0][tail:, 0:cols] = jnp.broadcast_to(flags[...].astype(F32), (PAD, cols)).astype(BF16)
    for copy in copies:
        copy.wait()


def side_by_side(block, first, cols, pair):
    at = slice(pair * LANES, (pair + 1) * LANES)
    pieces = [block[(first + r) * cols : (first + r + 1) * cols, at] for r in range(SIZE)]
    return jnp.concatenate(pieces, axis=1)


def write_shards(total, shards, depth_index):
    slots, cols, _ = total.shape
    count = len(shards)
    part = cols // count
    for k, shard in enumerate(shards):
        begin = pl.multiple_of(lax.bitwise_xor(depth_index, k) * part, part)
        for slot in range(slots):
            rows = total[slot, pl.ds(begin, part), :]
            shard[slot * part : (slot + 1) * part, :] = rows


def own_kernel(live, rows_in, gain, w_query, w_key, *rest, shards):
    normed_out, query_out = rest[0], rest[1]
    outs = rest[2 : 2 + shards]
    keys, total = rest[2 + shards :]
    groups, pairs = query_out.shape[0], query_out.shape[1]
    _, cols, width = rows_in.shape
    low = lax.broadcasted_iota(jnp.int32, (cols, LANES), 1) < LANES // 2
    zero = jnp.zeros((cols, LANES), BF16)
    local = w_query.shape[1]
    weights = jnp.concatenate([w_query[...], w_key[...]], axis=1)
    for g in range(groups):
        rows = rows_in[g * SIZE : (g + 1) * SIZE].reshape(SIZE * cols, width)
        normed = normed_rows(rows, gain[...])
        normed_out[g] = normed
        both_sides = dot(normed, weights)
        query, key = both_sides[:, :local], both_sides[:, local:].astype(BF16)
        for r in range(SIZE):
            scale = live[g * SIZE + r : g * SIZE + r + 1, :]
            for p in range(pairs):
                both = query[r * cols : (r + 1) * cols, p * LANES : (p + 1) * LANES]
                both = (both * scale).astype(BF16)
                at = slice(r * LANES, (r + 1) * LANES)
                query_out[g, p, 0:cols, at] = jnp.where(low, both, zero)
                query_out[g, p, cols : 2 * cols, at] = jnp.where(low, zero, both)
        for p in range(pairs):
            keys[g, p] = side_by_side(key, 0, cols, p)
    for p in range(pairs):
        score = dot_t(query_out[0, p], keys[0, p])
        for g in range(1, groups):
            score = score + dot_t(query_out[g, p], keys[g, p])
        total[2 * p] = score[:cols]
        total[2 * p + 1] = score[cols:]
    write_shards(total, outs, lax.axis_index("depth"))
    real = jnp.sum(live[...], axis=0, keepdims=True)
    for out in outs:
        out[out.shape[0] - 8 :, :] = jnp.broadcast_to(real, (8, LANES))


def value_kernel(*refs, cores, cols):
    parts = len(refs) - 2
    normed, w_value, values = refs[:parts], refs[parts], refs[parts + 1]
    _, inner, pairs, _, _ = values.shape
    each = inner * cores // parts
    for n in range(parts):
        value = dot(normed[n][...], w_value[...]).astype(BF16)
        for g in range(each):
            for p in range(pairs):
                block = side_by_side(value, g * SIZE, cols, p)
                values[n % cores, n // cores * each + g, p] = block


def own_value_kernel(normed, w_value, values, *, cols):
    for g in range(values.shape[0]):
        value = dot(normed[g], w_value[...]).astype(BF16)
        for p in range(values.shape[1]):
            values[g, p] = side_by_side(value, 0, cols, p)


def remote_kernel(part, gain, w_key, query, *rest, step, steps, chunk, part_cols, cores, shards):
    if step > 0:
        before, rest = rest[0], rest[1:]
    normed_out, rest = rest[0], rest[1:]
    last = step + 1 == steps
    used = normed_out.shape[0]
    rows, cols = used // part_cols, part_cols
    pairs, full = query.shape[1], query.shape[2] // 2
    normed = normed_rows(part[0:used, :], gain[...])
    normed_out[...] = normed
    key = dot(normed, w_key[...]).astype(BF16)
    total = rest[shards] if last else rest[0]
    inner = rows // SIZE
    source = lax.rem(lax.axis_index("heads") + cores - step % cores, cores)
    base = source * (steps // cores) * inner + step // cores * inner
    low = lax.broadcasted_iota(jnp.int32, (full, LANES), 1) < LANES // 2
    for p in range(pairs):
        score = before[p] if step > 0 else None
        whole = None
        for g in range(inner):
            one = side_by_side(key, g * SIZE, cols, p)
            twice = jnp.concatenate([one, one], axis=0)
            extra = dot_t(query[base + g, p], twice)
            whole = extra if whole is None else whole + extra
        left, right = whole[:full], whole[full:]
        if chunk % 2 == 1:
            left, right = right, left
        packed = jnp.where(low, left, right)
        total[p] = packed if score is None else score + packed
    if last:
        write_shards(total, rest[:shards], lax.axis_index("depth"))


def added(pieces):
    total = pieces[0][...]
    for piece in pieces[1:]:
        total = total + piece[...]
    return total


def diagonal(rows):
    row = lax.broadcasted_iota(jnp.int32, (rows, LANES), 0)
    return row == lax.broadcasted_iota(jnp.int32, (rows, LANES), 1)


def low_lanes(rows):
    return lax.broadcasted_iota(jnp.int32, (rows, LANES), 1) < LANES // 2


def half_mask(valid, half, rows):
    flags = valid[...]
    turned = pltpu.roll(flags, LANES // 2, 1)
    low = low_lanes(1)
    both = jnp.where(low, flags, turned) if half == 0 else jnp.where(low, turned, flags)
    return jnp.broadcast_to(both > 0.5, (rows, LANES))


def row_max(block):
    return jnp.max(block, axis=-1, keepdims=True)


def row_sum(block):
    return jnp.sum(block, axis=-1, keepdims=True)


def own_soft_kernel(*rest, shards, offsets, heads, head_width):
    valid, rest = rest[: 1 + offsets], rest[1 + offsets :]
    probs, stats = rest[-2:]
    sums = [added(rest[t * shards : (t + 1) * shards]) for t in range(1 + offsets)]
    rows = stats.shape[1]
    part = rows // heads
    factor = lax.rsqrt(F32(head_width) * sums[0][rows : rows + 1, 0:1])
    mask = jnp.broadcast_to(valid[0][...] > 0.5, (part, LANES))
    halves = [half_mask(valid[1 + o], 0, part) for o in range(offsets)]
    low = low_lanes(part)
    for p in range(heads // 2):
        at = slice(p * part, (p + 1) * part)
        near = []
        for o in range(offsets):
            near.append(jnp.where(halves[o], sums[1 + o][at] * factor, LOWEST))
        highest = functools.reduce(jnp.maximum, near)
        tops, wholes = [], []
        for h in (2 * p, 2 * p + 1):
            mine = slice(h * part, (h + 1) * part)
            side = low if h % 2 == 0 else jnp.logical_not(low)
            scaled = jnp.where(mask, sums[0][mine] * factor, LOWEST)
            top = row_max(jnp.maximum(scaled, jnp.where(side, highest, LOWEST)))
            expo = jnp.where(mask, jnp.exp(scaled - top), 0.0)
            probs[mine, :] = expo.astype(BF16)
            tops.append(top)
            wholes.append(expo)
        top = jnp.where(low, tops[0], tops[1])
        mass = jnp.zeros((part, LANES), F32)
        for o in range(offsets):
            expo = jnp.where(halves[o], jnp.exp(near[o] - top), 0.0)
            begin = rows + (o * heads // 2 + p) * part
            probs[begin : begin + part, :] = expo.astype(BF16)
            mass = mass + expo
        for h in (2 * p, 2 * p + 1):
            mine = slice(h * part, (h + 1) * part)
            side = low if h % 2 == 0 else jnp.logical_not(low)
            whole = row_sum(wholes[h % 2] + jnp.where(side, mass, 0.0))
            stats[0, mine, :] = jnp.broadcast_to(tops[h % 2], (part, LANES))
            stats[1, mine, :] = jnp.broadcast_to(whole, (part, LANES))
            stats[2, mine, :] = jnp.broadcast_to(factor, (part, LANES))


def last_soft_kernel(*rest, shards, offsets, heads):
    valid, stats, probs = rest[:offsets], rest[offsets], rest[-1]
    rest = rest[offsets + 1 : -1]
    sums = [added(rest[t * shards : (t + 1) * shards]) for t in range(offsets)]
    part = stats.shape[1] // heads
    low = low_lanes(part)
    halves = [half_mask(valid[o], 1, part) for o in range(offsets)]
    kept = diagonal(part)
    lines = []
    for p in range(heads // 2):
        at = slice(p * part, (p + 1) * part)
        factor = stats[2, 2 * p * part : (2 * p + 1) * part, :]
        far = [jnp.where(halves[o], sums[o][at] * factor, LOWEST) for o in range(offsets)]
        highest = functools.reduce(jnp.maximum, far)
        tops, shifts = [], []
        for h in (2 * p, 2 * p + 1):
            old = stats[0, h * part : (h + 1) * part, :]
            side = jnp.logical_not(low) if h % 2 == 0 else low
            top = jnp.maximum(old, row_max(jnp.where(side, highest, LOWEST)))
            tops.append(top)
            shifts.append(jnp.exp(old - top))
        top = jnp.where(low, tops[1], tops[0])
        expo = [jnp.where(halves[o], jnp.exp(far[o] - top), 0.0) for o in range(offsets)]
        mass = functools.reduce(jnp.add, expo)
        wholes = []
        for h in (2 * p, 2 * p + 1):
            side = jnp.logical_not(low) if h % 2 == 0 else low
            own = stats[1, h * part : (h + 1) * part, :]
            whole = shifts[h % 2] * own + row_sum(jnp.where(side, mass, 0.0))
            wholes.append(whole)
            block = jnp.where(kept, shifts[h % 2] / whole, 0.0)
            lines.append(jnp.sum(block, axis=0, keepdims=True))
        whole = jnp.where(low, wholes[1], wholes[0])
        for o in range(offsets):
            begin = (o * heads // 2 + p) * part
            probs[begin : begin + part, :] = (expo[o] / whole).astype(BF16)
    lines = jnp.concatenate(lines + [jnp.zeros((8 - heads, LANES), F32)], axis=0)
    coarse = lines.astype(BF16).astype(F32)
    tail = jnp.concatenate([coarse, lines - coarse], axis=0)
    probs[probs.shape[0] - PAD :, :] = tail.astype(BF16)


def collect(owns, others, probs, heads):
    blocks = probs.shape[2] // LANES
    cols = probs.shape[1] // 2
    part = (others[0].shape[0] - PAD) // ((blocks - 1) * heads // 2)
    kept = diagonal(part)
    low = low_lanes(part)
    for k in range(len(owns)):
        begin = lax.bitwise_xor(lax.axis_index("depth"), k) * part
        tail = others[k][others[k].shape[0] - PAD :, :].astype(F32)
        lines = tail[0:8] + tail[8:16]
        for head in range(heads):
            at = pl.ds(pl.multiple_of(head % 2 * cols + begin, part), part)
            line = jnp.where(kept, jnp.broadcast_to(lines[head : head + 1], (part, LANES)), 0.0)
            scale = row_sum(line)
            own = owns[k][head * part : (head + 1) * part, :].astype(F32) * scale
            probs[head // 2, at, 0:LANES] = own.astype(BF16)
            for o in range(blocks - 1):
                first = (o * heads // 2 + head // 2) * part
                near = owns[k][heads * part + first : heads * part + first + part, :]
                near = near.astype(F32) * scale
                far = others[k][first : first + part, :].astype(F32)
                if head % 2 == 0:
                    both = jnp.where(low, near, far)
                else:
                    both = pltpu.roll(jnp.where(low, far, near), LANES // 2, 1)
                probs[head // 2, at, (1 + o) * LANES : (2 + o) * LANES] = both.astype(BF16)


def mix_kernel(*rest, side, cores, tiles, shards, heads):
    if shards:
        rest, probs = rest[:-1], rest[-1]
        collect(rest[:shards], rest[shards : 2 * shards], probs, heads)
        rest = rest[2 * shards :]
    else:
        probs, rest = rest[0], rest[1:]
    own, remote, out = rest[0], rest[1 : 1 + tiles], rest[1 + tiles]
    _, pairs, cols, lanes = own.shape
    inner = own.shape[0] // cores
    low = jnp.concatenate([low_lanes(cols)] * (lanes // LANES), axis=1)
    step = lax.rem(lax.axis_index("heads") + cores - side, cores)
    for g in range(inner):
        for p in range(pairs):
            blocks = [own[side * inner + g, p]]
            blocks += [block[step, g, p] for block in remote]
            mixed = dot(probs[p], jnp.concatenate(blocks, axis=0))
            picked = jnp.where(low, mixed[:cols], mixed[cols:]).astype(BF16)
            for r in range(SIZE):
                at = slice(r * LANES, (r + 1) * LANES)
                out[g * SIZE + r, :, p * LANES : (p + 1) * LANES] = picked[:, at]


def order_kernel(w_out, ordered, *, cores):
    local = w_out.shape[0] // cores
    for k in range(cores):
        source = lax.rem(lax.axis_index("heads") + cores - k, cores)
        rows = w_out[pl.ds(pl.multiple_of(source * local, local), local), :]
        ordered[k * local : (k + 1) * local, :] = rows


def projected(live, parts, weights, first):
    size, cols, local = parts[0].shape
    blocks = [part[...].reshape(size * cols, local) for part in parts]
    total = dot(jnp.concatenate(blocks, axis=1), weights[...])
    results = []
    for r in range(size):
        scale = live[first + r : first + r + 1, :]
        scale = jnp.concatenate([scale] * (total.shape[1] // LANES), axis=1)
        results.append((total[r * cols : (r + 1) * cols] * scale).astype(BF16))
    return results


def project_kernel(live, *rest, cores, first):
    parts, weights, out = rest[:cores], rest[cores], rest[cores + 1]
    for r, rows in enumerate(projected(live, parts, weights, first)):
        out[r] = rows


def finish_kernel(live, *rest, cores):
    parts, weights, ready = rest[:cores], rest[cores], rest[cores + 1 : -3]
    out, buffer, sems = rest[-3:]
    size = buffer.shape[0]
    copies = []
    for k, done in enumerate(ready):
        copies.append(pltpu.make_async_copy(done, out.at[pl.ds(k * size, size)], sems.at[k]))
        copies[-1].start()
    first = len(ready) * size
    for r, rows in enumerate(projected(live, parts, weights, first)):
        buffer[r] = rows
        at = out.at[first + r]
        copies.append(pltpu.make_async_copy(buffer.at[r], at, sems.at[len(ready) + r]))
        copies[-1].start()
    for copy in copies:
        copy.wait()


def on_device(alignment, norm_gain, w_query, w_key, w_value, w_out, row_mask, col_valid):
    rows_here, cols_here, width = alignment.shape
    local_width = w_query.shape[1]
    head_width = width // HEADS
    local_heads = local_width // head_width
    pairs = local_heads // 2
    offsets = lax.axis_size("cols") - 1
    depth = lax.axis_size("depth")
    cores = lax.axis_size("heads")
    core = lax.axis_index("heads")
    part_rows = rows_here // cores
    inner = part_rows // SIZE
    groups = rows_here // SIZE
    part_cols = cols_here // CHUNKS
    direct = depth in (2, 4, 8) and cols_here % (16 * depth) == 0
    shards = depth if direct else 1
    part = cols_here // shards
    lanes = SIZE * LANES
    total_cols = (1 + offsets) * cols_here
    shape = jax.ShapeDtypeStruct
    gain = norm_gain[None, :]
    live = jnp.broadcast_to(row_mask.astype(F32)[:, None], (rows_here, LANES))

    first = lax.dynamic_slice(
        alignment, (core * part_rows, 0, 0), (part_rows, cols_here - part_cols, width)
    )
    sent = {(0, 0): first.reshape(part_rows * part_cols, width)}
    spans = [1] * CHUNKS
    some = part_rows // spans[-1] * part_cols
    resident, *lasts = call(
        functools.partial(load_kernel, part_cols=part_cols),
        [shape((rows_here, cols_here, width), BF16), shape((some + PAD, width), BF16)]
        + [shape((some, width), BF16)] * (spans[-1] - 1),
        [spec(HBM), spec(HBM)],
        [
            pltpu.VMEM((1, cols_here), jnp.int32),
            pltpu.SemaphoreType.DMA((part_rows + rows_here + 1,)),
        ],
    )(col_valid[None, :], alignment)
    for m, block in enumerate(lasts):
        sent[CHUNKS - 1, m] = block
    arrived = {}
    for offset in range(1, offsets + 1):
        for (c, m), block in sent.items():
            mine = from_behind(block, "cols", offset)
            arrived[offset, c, m] = [mine] + [
                from_behind(mine, "heads", k) for k in range(1, cores)
            ]

    def exchange(values):
        received = [values[0]]
        for k in range(1, shards):
            swapped = [(source, source ^ k) for source in range(depth)]
            received.append(lax.ppermute(values[k], "depth", swapped))
        return received

    own = call(
        functools.partial(own_kernel, shards=shards),
        [
            shape((groups, SIZE * cols_here, width), BF16),
            shape((groups, pairs, 2 * cols_here, lanes), BF16),
        ]
        + [shape((local_heads * part + 8, cols_here), F32)] * shards,
        [spec()] * 5,
        [
            pltpu.VMEM((groups, pairs, cols_here, lanes), BF16),
            pltpu.VMEM((local_heads, cols_here, cols_here), F32),
        ],
        flops=4 * rows_here * cols_here * width * local_width,
    )(live, resident, gain, w_query, w_key)
    normed, query, own_sums = own[0], own[1], exchange(own[2:])

    own_values = call(
        functools.partial(own_value_kernel, cols=cols_here),
        shape((groups, pairs, cols_here, lanes), BF16),
        [spec()] * 2,
        flops=2 * rows_here * cols_here * width * local_width,
    )(normed, w_value)
    ordered = call(
        functools.partial(order_kernel, cores=cores), shape(w_out.shape, BF16), [spec()]
    )(w_out)

    tiles, remote_values = [], []
    for offset in range(1, offsets + 1):
        for c in range(CHUNKS):
            before, rows_of = [], []
            steps = spans[c] * cores
            used = part_rows // spans[c] * part_cols
            for n in range(steps):
                m, k = divmod(n, cores)
                outs = [shape((used, width), BF16)]
                scratch = []
                if n + 1 == steps:
                    outs += [shape((pairs * part, LANES), F32)] * shards
                    scratch = [pltpu.VMEM((pairs, cols_here, LANES), F32)]
                else:
                    outs += [shape((pairs, cols_here, LANES), F32)]
                result = call(
                    functools.partial(
                        remote_kernel,
                        step=n,
                        steps=steps,
                        chunk=c,
                        part_cols=part_cols,
                        cores=cores,
                        shards=shards,
                    ),
                    outs,
                    [spec()] * (4 + len(before)),
                    scratch,
                    flops=2 * used * width * local_width,
                )(arrived[offset, c, m][k], gain, w_key, query, *before)
                rows_of.append(result[0])
                before = [result[1]]
            tiles.append(exchange(result[1:]))
            remote_values.append(
                call(
                    functools.partial(value_kernel, cores=cores, cols=part_cols),
                    shape((cores, inner, pairs, part_cols, lanes), BF16),
                    [spec()] * (steps + 1),
                    flops=2 * cores * part_rows * part_cols * width * local_width,
                )(*rows_of, w_value)
            )

    valid_tiles = [col_valid.astype(BF16)[None, :]]
    for offset in range(1, offsets + 1):
        valid_tiles.append(arrived[offset, CHUNKS - 1, 0][0][-PAD : 1 - PAD, :cols_here])
    if direct:
        valid = [tile.astype(F32) for tile in valid_tiles]
        rows = local_heads * part
        far_rows = offsets * pairs * part
        early = [piece for tile in tiles[0::CHUNKS] for piece in tile]
        late = [piece for tile in tiles[1::CHUNKS] for piece in tile]
        own_probs, stats = call(
            functools.partial(
                own_soft_kernel,
                shards=shards,
                offsets=offsets,
                heads=local_heads,
                head_width=head_width,
            ),
            [shape((rows + far_rows, LANES), BF16), shape((3, rows, LANES), F32)],
            [spec()] * ((1 + offsets) * (1 + shards)),
            flops=1000000,
        )(*valid, *own_sums, *early)
        own_probs = exchange([own_probs] * shards)
        probs = call(
            functools.partial(
                last_soft_kernel, shards=shards, offsets=offsets, heads=local_heads
            ),
            shape((far_rows + PAD, LANES), BF16),
            [spec()] * (1 + offsets * (1 + shards)),
            flops=1000000,
        )(*valid[1:], stats, *late)
        probs = exchange([probs] * shards)
        probs = own_probs + probs
    else:
        count = lax.psum(jnp.sum(row_mask.astype(F32)), "depth")
        own_part = own_sums[0][: local_heads * cols_here]
        blocks = [own_part.reshape(local_heads, cols_here, cols_here)]
        for index, tile in enumerate(tiles):
            packed = tile[0].reshape(pairs, cols_here, 2, part_cols)
            packed = packed[:, :, ::-1] if index % CHUNKS % 2 == 1 else packed
            packed = jnp.transpose(packed, (0, 2, 1, 3))
            blocks.append(packed.reshape(local_heads, cols_here, part_cols))
        logits = jnp.concatenate(blocks, axis=2)
        share = lax.psum_scatter(logits, "depth", scatter_dimension=1, tiled=True)
        mask = jnp.concatenate(valid_tiles, axis=1)[None] > 0.5
        scaled = jnp.where(mask, share * lax.rsqrt(F32(head_width) * count), LOWEST)
        expo = jnp.where(mask, jnp.exp(scaled - jnp.max(scaled, axis=-1, keepdims=True)), 0.0)
        probs = (expo / jnp.sum(expo, axis=-1, keepdims=True)).astype(BF16)
        probs = lax.all_gather(probs, "depth", axis=1, tiled=True)
        probs = [probs.reshape(pairs, 2 * cols_here, total_cols)]

    finished = []
    piece = shape((part_rows, cols_here, local_width), BF16)
    for side in range(cores):
        gathers = len(probs) // 2
        outs = [piece]
        if gathers:
            outs.append(shape((pairs, 2 * cols_here, total_cols), BF16))
        mixed = call(
            functools.partial(
                mix_kernel,
                side=side,
                cores=cores,
                tiles=len(tiles),
                shards=gathers,
                heads=local_heads,
            ),
            outs,
            [spec()] * (len(probs) + 1 + len(remote_values)),
            flops=4 * SIZE * cols_here * total_cols * local_width,
        )(*probs, own_values, *remote_values)
        mine, probs = mixed[0], mixed[1:] if gathers else probs
        parts = [mine] + [from_behind(mine, "heads", k) for k in range(1, cores)]
        if side + 1 < cores:
            finished.append(
                call(
                    functools.partial(project_kernel, cores=cores, first=side * part_rows),
                    piece,
                    [spec()] * (cores + 2),
                    flops=2 * SIZE * cols_here * width * local_width,
                )(live, *parts, ordered)
            )
    return call(
        functools.partial(finish_kernel, cores=cores),
        shape((rows_here, cols_here, local_width), BF16),
        [spec()] * (2 * cores + 1),
        [
            pltpu.VMEM((part_rows, cols_here, local_width), BF16),
            pltpu.SemaphoreType.DMA((cores - 1 + part_rows,)),
        ],
        flops=2 * SIZE * cols_here * width * local_width,
        space=HBM,
    )(live, *parts, ordered, *finished)


def solution(mesh):
    in_specs = (
        P(("groups", "depth"), "cols", None),
        P(),
        P(None, "heads"),
        P(None, "heads"),
        P(None, "heads"),
        P(None, "heads"),
        P(("groups", "depth")),
        P(("groups", "cols")),
    )
    out_specs = P(("groups", "depth"), "cols", "heads")

    return jax.shard_map(
        on_device, mesh=mesh, in_specs=in_specs, out_specs=out_specs, check_vma=False
    )
```

```python
import functools

import jax
import jax.numpy as jnp
from jax import lax
from jax.experimental import pallas as pl
from jax.experimental.pallas import tpu as pltpu
from jax.sharding import PartitionSpec as P

HEADS = 12
LANES = 128
CHUNKS = 2
SIZE = 2
LIMIT = 16 << 20
LOWEST = -1e30
PAD = 16


VMEM = pltpu.VMEM
SMEM = pltpu.SMEM
HBM = pltpu.HBM
BF16 = jnp.bfloat16
F32 = jnp.float32


def from_behind(value, axis, steps):
    count = lax.axis_size(axis)
    return lax.ppermute(value, axis, [(s, (s + steps) % count) for s in range(count)])


def spec(space=VMEM):
    return pl.BlockSpec(memory_space=space)


def call(kernel, out_shape, in_specs, scratch=(), flops=0, space=VMEM):
    single = not isinstance(out_shape, (list, tuple))
    shapes = [out_shape] if single else list(out_shape)
    nbytes = sum(s.size * s.dtype.itemsize for s in shapes)
    shapes = [space(s.shape, s.dtype) for s in shapes]
    fn = pl.pallas_call(
        kernel,
        out_shape=shapes,
        in_specs=in_specs,
        out_specs=[spec(space) for _ in shapes],
        scratch_shapes=list(scratch),
        compiler_params=pltpu.CompilerParams(vmem_limit_bytes=LIMIT),
        cost_estimate=pl.CostEstimate(flops=flops, transcendentals=0, bytes_accessed=2 * nbytes),
    )

    def run(*args):
        args = [
            arg
            if block.memory_space == SMEM
            else pltpu.with_memory_space_constraint(arg, block.memory_space)
            for arg, block in zip(args, in_specs, strict=True)
        ]
        out = fn(*args)
        return out[0] if single else out

    return run


def dot(left, right):
    return jnp.dot(left, right, preferred_element_type=F32)


def dot_t(left, right):
    return lax.dot_general(left, right, (((1,), (1,)), ((), ())), preferred_element_type=F32)


def normed_rows(rows, gain):
    values_f = rows.astype(F32)
    average = jnp.mean(values_f, axis=-1, keepdims=True)
    centred = values_f - average
    spread = jnp.mean(centred * centred, axis=-1, keepdims=True)
    return (centred * lax.rsqrt(spread + 1e-05) * gain).astype(BF16)


def load_kernel(valid, rows_in, resident, *rest, part_cols):
    lasts, flags, sems = rest[:-2], rest[-2], rest[-1]
    rows_here, cols, _ = resident.shape
    some = lasts[-1].shape[0] // part_cols
    begin = lax.axis_index("heads") * some * len(lasts)
    first = pltpu.make_async_copy(valid, flags, sems.at[rows_here + some * len(lasts)])
    first.start()
    copies = []
    for r in range(some * len(lasts)):
        source = rows_in.at[begin + r, pl.ds(cols - part_cols, part_cols), :]
        target = lasts[r // some].at[pl.ds(r % some * part_cols, part_cols)]
        copies.append(pltpu.make_async_copy(source, target, sems.at[rows_here + r]))
    for r in range(rows_here):
        copies.append(pltpu.make_async_copy(rows_in.at[r], resident.at[r], sems.at[r]))
    for copy in copies:
        copy.start()
    first.wait()
    tail = some * part_cols
    lasts[0][tail:, :] = jnp.zeros((PAD, lasts[0].shape[1]), BF16)
    lasts[0][tail:, 0:cols] = jnp.broadcast_to(flags[...].astype(F32), (PAD, cols)).astype(BF16)
    for copy in copies:
        copy.wait()


def side_by_side(block, first, cols, pair):
    at = slice(pair * LANES, (pair + 1) * LANES)
    pieces = [block[(first + r) * cols : (first + r + 1) * cols, at] for r in range(SIZE)]
    return jnp.concatenate(pieces, axis=1)


def write_shards(total, shards, depth_index):
    slots, cols, _ = total.shape
    count = len(shards)
    part = cols // count
    for k, shard in enumerate(shards):
        begin = lax.bitwise_xor(depth_index, k) * part if count > 1 else 0
        for slot in range(slots):
            rows = total[slot, pl.ds(pl.multiple_of(begin, part), part), :]
            shard[slot * part : (slot + 1) * part, :] = rows


def own_kernel(live, rows_in, gain, w_query, w_key, *rest, shards):
    normed_out, query_out = rest[0], rest[1]
    outs = rest[2 : 2 + shards]
    keys, total = rest[2 + shards :]
    groups, pairs = query_out.shape[0], query_out.shape[1]
    _, cols, width = rows_in.shape
    low = lax.broadcasted_iota(jnp.int32, (cols, LANES), 1) < LANES // 2
    zero = jnp.zeros((cols, LANES), BF16)
    local = w_query.shape[1]
    weights = jnp.concatenate([w_query[...], w_key[...]], axis=1)
    for g in range(groups):
        rows = rows_in[g * SIZE : (g + 1) * SIZE].reshape(SIZE * cols, width)
        normed = normed_rows(rows, gain[...])
        normed_out[g] = normed
        both_sides = dot(normed, weights)
        query, key = both_sides[:, :local], both_sides[:, local:].astype(BF16)
        for r in range(SIZE):
            scale = live[g * SIZE + r : g * SIZE + r + 1, :]
            for p in range(pairs):
                both = query[r * cols : (r + 1) * cols, p * LANES : (p + 1) * LANES]
                both = (both * scale).astype(BF16)
                at = slice(r * LANES, (r + 1) * LANES)
                query_out[g, p, 0:cols, at] = jnp.where(low, both, zero)
                query_out[g, p, cols : 2 * cols, at] = jnp.where(low, zero, both)
        for p in range(pairs):
            keys[g, p] = side_by_side(key, 0, cols, p)
    for p in range(pairs):
        score = dot_t(query_out[0, p], keys[0, p])
        for g in range(1, groups):
            score = score + dot_t(query_out[g, p], keys[g, p])
        total[2 * p] = score[:cols]
        total[2 * p + 1] = score[cols:]
    write_shards(total, outs, lax.axis_index("depth"))
    real = jnp.sum(live[...], axis=0, keepdims=True)
    for out in outs:
        out[out.shape[0] - 8 :, :] = jnp.broadcast_to(real, (8, LANES))


def value_kernel(*refs, cores, cols):
    parts = len(refs) - 2
    normed, w_value, values = refs[:parts], refs[parts], refs[parts + 1]
    _, inner, pairs, _, _ = values.shape
    each = inner * cores // parts
    for n in range(parts):
        value = dot(normed[n][...], w_value[...]).astype(BF16)
        for g in range(each):
            for p in range(pairs):
                block = side_by_side(value, g * SIZE, cols, p)
                values[n % cores, n // cores * each + g, p] = block


def own_value_kernel(normed, w_value, values, *, cols):
    for g in range(values.shape[0]):
        value = dot(normed[g], w_value[...]).astype(BF16)
        for p in range(values.shape[1]):
            values[g, p] = side_by_side(value, 0, cols, p)


def remote_kernel(part, gain, w_key, query, *rest, step, steps, chunk, part_cols, cores, shards):
    if step > 0:
        before, rest = rest[0], rest[1:]
    normed_out, rest = rest[0], rest[1:]
    last = step + 1 == steps
    used = normed_out.shape[0]
    rows, cols = used // part_cols, part_cols
    pairs, full = query.shape[1], query.shape[2] // 2
    normed = normed_rows(part[0:used, :], gain[...])
    normed_out[...] = normed
    key = dot(normed, w_key[...]).astype(BF16)
    total = rest[shards] if last else rest[0]
    inner = rows // SIZE
    source = lax.rem(lax.axis_index("heads") + cores - step % cores, cores)
    base = source * (steps // cores) * inner + step // cores * inner
    low = lax.broadcasted_iota(jnp.int32, (full, LANES), 1) < LANES // 2
    for p in range(pairs):
        score = before[p] if step > 0 else None
        whole = None
        for g in range(inner):
            one = side_by_side(key, g * SIZE, cols, p)
            twice = jnp.concatenate([one, one], axis=0)
            extra = dot_t(query[base + g, p], twice)
            whole = extra if whole is None else whole + extra
        left, right = whole[:full], whole[full:]
        if chunk % 2 == 1:
            left, right = right, left
        packed = jnp.where(low, left, right)
        total[p] = packed if score is None else score + packed
    if last:
        write_shards(total, rest[:shards], lax.axis_index("depth"))


def added(pieces):
    total = pieces[0][...]
    for piece in pieces[1:]:
        total = total + piece[...]
    return total


def diagonal(rows):
    row = lax.broadcasted_iota(jnp.int32, (rows, LANES), 0)
    return row == lax.broadcasted_iota(jnp.int32, (rows, LANES), 1)


def low_lanes(rows):
    return lax.broadcasted_iota(jnp.int32, (rows, LANES), 1) < LANES // 2


def half_mask(valid, half, rows):
    flags = valid[...]
    turned = pltpu.roll(flags, LANES // 2, 1)
    low = low_lanes(1)
    both = jnp.where(low, flags, turned) if half == 0 else jnp.where(low, turned, flags)
    return jnp.broadcast_to(both > 0.5, (rows, LANES))


def row_max(block):
    return jnp.max(block, axis=-1, keepdims=True)


def row_sum(block):
    return jnp.sum(block, axis=-1, keepdims=True)


def own_soft_kernel(*rest, shards, offsets, heads, head_width):
    valid, rest = rest[: 1 + offsets], rest[1 + offsets :]
    probs, stats = rest[-2:]
    sums = [added(rest[t * shards : (t + 1) * shards]) for t in range(1 + offsets)]
    rows = stats.shape[1]
    part = rows // heads
    factor = lax.rsqrt(F32(head_width) * sums[0][rows : rows + 1, 0:1])
    mask = jnp.broadcast_to(valid[0][...] > 0.5, (part, LANES))
    halves = [half_mask(valid[1 + o], 0, part) for o in range(offsets)]
    low = low_lanes(part)
    for p in range(heads // 2):
        at = slice(p * part, (p + 1) * part)
        near = []
        for o in range(offsets):
            near.append(jnp.where(halves[o], sums[1 + o][at] * factor, LOWEST))
        highest = functools.reduce(jnp.maximum, near)
        tops, wholes = [], []
        for h in (2 * p, 2 * p + 1):
            mine = slice(h * part, (h + 1) * part)
            side = low if h % 2 == 0 else jnp.logical_not(low)
            scaled = jnp.where(mask, sums[0][mine] * factor, LOWEST)
            top = row_max(jnp.maximum(scaled, jnp.where(side, highest, LOWEST)))
            expo = jnp.where(mask, jnp.exp(scaled - top), 0.0)
            probs[mine, :] = expo.astype(BF16)
            tops.append(top)
            wholes.append(expo)
        top = jnp.where(low, tops[0], tops[1])
        mass = jnp.zeros((part, LANES), F32)
        for o in range(offsets):
            expo = jnp.where(halves[o], jnp.exp(near[o] - top), 0.0)
            begin = rows + (o * heads // 2 + p) * part
            probs[begin : begin + part, :] = expo.astype(BF16)
            mass = mass + expo
        for h in (2 * p, 2 * p + 1):
            mine = slice(h * part, (h + 1) * part)
            side = low if h % 2 == 0 else jnp.logical_not(low)
            whole = row_sum(wholes[h % 2] + jnp.where(side, mass, 0.0))
            stats[0, mine, :] = jnp.broadcast_to(tops[h % 2], (part, LANES))
            stats[1, mine, :] = jnp.broadcast_to(whole, (part, LANES))
            stats[2, mine, :] = jnp.broadcast_to(factor, (part, LANES))


def last_soft_kernel(*rest, shards, offsets, heads):
    valid, stats, probs = rest[:offsets], rest[offsets], rest[-1]
    rest = rest[offsets + 1 : -1]
    sums = [added(rest[t * shards : (t + 1) * shards]) for t in range(offsets)]
    part = stats.shape[1] // heads
    low = low_lanes(part)
    halves = [half_mask(valid[o], 1, part) for o in range(offsets)]
    kept = diagonal(part)
    lines = []
    for p in range(heads // 2):
        at = slice(p * part, (p + 1) * part)
        factor = stats[2, 2 * p * part : (2 * p + 1) * part, :]
        far = [jnp.where(halves[o], sums[o][at] * factor, LOWEST) for o in range(offsets)]
        highest = functools.reduce(jnp.maximum, far)
        tops, shifts = [], []
        for h in (2 * p, 2 * p + 1):
            old = stats[0, h * part : (h + 1) * part, :]
            side = jnp.logical_not(low) if h % 2 == 0 else low
            top = jnp.maximum(old, row_max(jnp.where(side, highest, LOWEST)))
            tops.append(top)
            shifts.append(jnp.exp(old - top))
        top = jnp.where(low, tops[1], tops[0])
        expo = [jnp.where(halves[o], jnp.exp(far[o] - top), 0.0) for o in range(offsets)]
        mass = functools.reduce(jnp.add, expo)
        wholes = []
        for h in (2 * p, 2 * p + 1):
            side = jnp.logical_not(low) if h % 2 == 0 else low
            own = stats[1, h * part : (h + 1) * part, :]
            whole = shifts[h % 2] * own + row_sum(jnp.where(side, mass, 0.0))
            wholes.append(whole)
            block = jnp.where(kept, shifts[h % 2] / whole, 0.0)
            lines.append(jnp.sum(block, axis=0, keepdims=True))
        whole = jnp.where(low, wholes[1], wholes[0])
        for o in range(offsets):
            begin = (o * heads // 2 + p) * part
            probs[begin : begin + part, :] = (expo[o] / whole).astype(BF16)
    lines = jnp.concatenate(lines + [jnp.zeros((8 - heads, LANES), F32)], axis=0)
    coarse = lines.astype(BF16).astype(F32)
    tail = jnp.concatenate([coarse, lines - coarse], axis=0)
    probs[probs.shape[0] - PAD :, :] = tail.astype(BF16)


def collect(owns, others, probs, heads):
    blocks = probs.shape[2] // LANES
    cols = probs.shape[1] // 2
    part = (others[0].shape[0] - PAD) // ((blocks - 1) * heads // 2)
    kept = diagonal(part)
    low = low_lanes(part)
    for k in range(len(owns)):
        begin = lax.bitwise_xor(lax.axis_index("depth"), k) * part
        tail = others[k][others[k].shape[0] - PAD :, :].astype(F32)
        lines = tail[0:8] + tail[8:16]
        for head in range(heads):
            at = pl.ds(pl.multiple_of(head % 2 * cols + begin, part), part)
            line = jnp.where(kept, jnp.broadcast_to(lines[head : head + 1], (part, LANES)), 0.0)
            scale = row_sum(line)
            own = owns[k][head * part : (head + 1) * part, :].astype(F32) * scale
            probs[head // 2, at, 0:LANES] = own.astype(BF16)
            for o in range(blocks - 1):
                first = (o * heads // 2 + head // 2) * part
                near = owns[k][heads * part + first : heads * part + first + part, :]
                near = near.astype(F32) * scale
                far = others[k][first : first + part, :].astype(F32)
                if head % 2 == 0:
                    both = jnp.where(low, near, far)
                else:
                    both = pltpu.roll(jnp.where(low, far, near), LANES // 2, 1)
                probs[head // 2, at, (1 + o) * LANES : (2 + o) * LANES] = both.astype(BF16)


def mix_kernel(*rest, side, cores, tiles, shards, heads):
    if shards:
        rest, probs = rest[:-1], rest[-1]
        collect(rest[:shards], rest[shards : 2 * shards], probs, heads)
        rest = rest[2 * shards :]
    else:
        probs, rest = rest[0], rest[1:]
    own, remote, out = rest[0], rest[1 : 1 + tiles], rest[1 + tiles]
    _, pairs, cols, lanes = own.shape
    inner = own.shape[0] // cores
    low = jnp.concatenate([low_lanes(cols)] * (lanes // LANES), axis=1)
    step = lax.rem(lax.axis_index("heads") + cores - side, cores)
    for g in range(inner):
        for p in range(pairs):
            blocks = [own[side * inner + g, p]]
            blocks += [block[step, g, p] for block in remote]
            mixed = dot(probs[p], jnp.concatenate(blocks, axis=0))
            picked = jnp.where(low, mixed[:cols], mixed[cols:]).astype(BF16)
            for r in range(SIZE):
                at = slice(r * LANES, (r + 1) * LANES)
                out[g * SIZE + r, :, p * LANES : (p + 1) * LANES] = picked[:, at]


def order_kernel(w_out, ordered, *, cores):
    local = w_out.shape[0] // cores
    for k in range(cores):
        source = lax.rem(lax.axis_index("heads") + cores - k, cores)
        rows = w_out[pl.ds(pl.multiple_of(source * local, local), local), :]
        ordered[k * local : (k + 1) * local, :] = rows


def mine_kernel(*rest):
    parts, weights, out = rest[:-2], rest[-2], rest[-1]
    size, cols, local = parts[0].shape
    for side, part in enumerate(parts):
        rows = part[...].reshape(size * cols, local)
        total = dot(rows, weights[0:local, :])
        out[side * size : (side + 1) * size] = total.reshape(size, cols, local)


def projected(live, half, parts, weights, begin, first):
    cols, local = parts[0].shape[1], parts[0].shape[2]
    blocks = [part[begin : begin + SIZE].reshape(SIZE * cols, local) for part in parts]
    block = jnp.concatenate(blocks, axis=1) if len(blocks) > 1 else blocks[0]
    at = first + begin
    total = dot(block, weights[local:, :]) + half[at : at + SIZE].reshape(SIZE * cols, local)
    results = []
    for r in range(SIZE):
        scale = live[at + r : at + r + 1, :]
        scale = jnp.concatenate([scale] * (local // LANES), axis=1)
        results.append((total[r * cols : (r + 1) * cols] * scale).astype(BF16))
    return results


def project_kernel(live, half, *rest, first):
    parts, weights, out = rest[:-2], rest[-2], rest[-1]
    for begin in range(0, out.shape[0], SIZE):
        for r, rows in enumerate(projected(live, half, parts, weights, begin, first)):
            out[begin + r] = rows


def finish_kernel(live, half, *rest, cores):
    parts, weights, ready = rest[: cores - 1], rest[cores - 1], rest[cores:-3]
    out, buffer, sems = rest[-3:]
    size = buffer.shape[0]
    copies = []
    for k, done in enumerate(ready):
        copies.append(pltpu.make_async_copy(done, out.at[pl.ds(k * size, size)], sems.at[k]))
        copies[-1].start()
    first = len(ready) * size
    for begin in range(0, size, SIZE):
        for r, rows in enumerate(projected(live, half, parts, weights, begin, first)):
            row = begin + r
            buffer[row] = rows
            target = out.at[first + row]
            copies.append(pltpu.make_async_copy(buffer.at[row], target, sems.at[len(ready) + row]))
            copies[-1].start()
    for copy in copies:
        copy.wait()


def on_device(alignment, norm_gain, w_query, w_key, w_value, w_out, row_mask, col_valid):
    rows_here, cols_here, width = alignment.shape
    local_width = w_query.shape[1]
    head_width = width // HEADS
    local_heads = local_width // head_width
    pairs = local_heads // 2
    offsets = lax.axis_size("cols") - 1
    depth = lax.axis_size("depth")
    cores = lax.axis_size("heads")
    core = lax.axis_index("heads")
    part_rows = rows_here // cores
    inner = part_rows // SIZE
    groups = rows_here // SIZE
    part_cols = cols_here // CHUNKS
    direct = depth in (2, 4, 8) and cols_here % (16 * depth) == 0
    shards = depth if direct else 1
    part = cols_here // shards
    lanes = SIZE * LANES
    total_cols = (1 + offsets) * cols_here
    shape = jax.ShapeDtypeStruct
    gain = norm_gain[None, :]
    live = jnp.broadcast_to(row_mask.astype(F32)[:, None], (rows_here, LANES))

    first = lax.dynamic_slice(
        alignment, (core * part_rows, 0, 0), (part_rows, cols_here - part_cols, width)
    )
    sent = {(0, 0): first.reshape(part_rows * part_cols, width)}
    spans = [1] * CHUNKS
    some = part_rows // spans[-1] * part_cols
    resident, *lasts = call(
        functools.partial(load_kernel, part_cols=part_cols),
        [shape((rows_here, cols_here, width), BF16), shape((some + PAD, width), BF16)]
        + [shape((some, width), BF16)] * (spans[-1] - 1),
        [spec(HBM), spec(HBM)],
        [
            pltpu.VMEM((1, cols_here), jnp.int32),
            pltpu.SemaphoreType.DMA((part_rows + rows_here + 1,)),
        ],
    )(col_valid[None, :], alignment)
    for m, block in enumerate(lasts):
        sent[CHUNKS - 1, m] = block
    arrived = {}
    for offset in range(1, offsets + 1):
        for (c, m), block in sent.items():
            mine = from_behind(block, "cols", offset)
            arrived[offset, c, m] = [mine] + [
                from_behind(mine, "heads", k) for k in range(1, cores)
            ]

    def exchange(values):
        received = [values[0]]
        for k in range(1, shards):
            swapped = [(source, source ^ k) for source in range(depth)]
            received.append(lax.ppermute(values[k], "depth", swapped))
        return received

    own = call(
        functools.partial(own_kernel, shards=shards),
        [
            shape((groups, SIZE * cols_here, width), BF16),
            shape((groups, pairs, 2 * cols_here, lanes), BF16),
        ]
        + [shape((local_heads * part + 8, cols_here), F32)] * shards,
        [spec()] * 5,
        [
            pltpu.VMEM((groups, pairs, cols_here, lanes), BF16),
            pltpu.VMEM((local_heads, cols_here, cols_here), F32),
        ],
        flops=4 * rows_here * cols_here * width * local_width,
    )(live, resident, gain, w_query, w_key)
    normed, query, own_sums = own[0], own[1], exchange(own[2:])

    own_values = call(
        functools.partial(own_value_kernel, cols=cols_here),
        shape((groups, pairs, cols_here, lanes), BF16),
        [spec()] * 2,
        flops=2 * rows_here * cols_here * width * local_width,
    )(normed, w_value)
    ordered = call(
        functools.partial(order_kernel, cores=cores), shape(w_out.shape, BF16), [spec()]
    )(w_out)

    tiles, remote_values = [], []
    for offset in range(1, offsets + 1):
        for c in range(CHUNKS):
            before, rows_of = [], []
            steps = spans[c] * cores
            used = part_rows // spans[c] * part_cols
            for n in range(steps):
                m, k = divmod(n, cores)
                outs = [shape((used, width), BF16)]
                scratch = []
                if n + 1 == steps:
                    outs += [shape((pairs * part, LANES), F32)] * shards
                    scratch = [pltpu.VMEM((pairs, cols_here, LANES), F32)]
                else:
                    outs += [shape((pairs, cols_here, LANES), F32)]
                result = call(
                    functools.partial(
                        remote_kernel,
                        step=n,
                        steps=steps,
                        chunk=c,
                        part_cols=part_cols,
                        cores=cores,
                        shards=shards,
                    ),
                    outs,
                    [spec()] * (4 + len(before)),
                    scratch,
                    flops=2 * used * width * local_width,
                )(arrived[offset, c, m][k], gain, w_key, query, *before)
                rows_of.append(result[0])
                before = [result[1]]
            tiles.append(exchange(result[1:]))
            remote_values.append(
                call(
                    functools.partial(value_kernel, cores=cores, cols=part_cols),
                    shape((cores, inner, pairs, part_cols, lanes), BF16),
                    [spec()] * (steps + 1),
                    flops=2 * cores * part_rows * part_cols * width * local_width,
                )(*rows_of, w_value)
            )

    valid_tiles = [col_valid.astype(BF16)[None, :]]
    for offset in range(1, offsets + 1):
        valid_tiles.append(arrived[offset, CHUNKS - 1, 0][0][-PAD : 1 - PAD, :cols_here])
    if direct:
        valid = [tile.astype(F32) for tile in valid_tiles]
        rows = local_heads * part
        far_rows = offsets * pairs * part
        early = [piece for tile in tiles[0::CHUNKS] for piece in tile]
        late = [piece for tile in tiles[1::CHUNKS] for piece in tile]
        own_probs, stats = call(
            functools.partial(
                own_soft_kernel,
                shards=shards,
                offsets=offsets,
                heads=local_heads,
                head_width=head_width,
            ),
            [shape((rows + far_rows, LANES), BF16), shape((3, rows, LANES), F32)],
            [spec()] * ((1 + offsets) * (1 + shards)),
            flops=1000000,
        )(*valid, *own_sums, *early)
        own_probs = exchange([own_probs] * shards)
        probs = call(
            functools.partial(
                last_soft_kernel, shards=shards, offsets=offsets, heads=local_heads
            ),
            shape((far_rows + PAD, LANES), BF16),
            [spec()] * (1 + offsets * (1 + shards)),
            flops=1000000,
        )(*valid[1:], stats, *late)
        probs = exchange([probs] * shards)
        probs = own_probs + probs
    else:
        count = lax.psum(jnp.sum(row_mask.astype(F32)), "depth")
        own_part = own_sums[0][: local_heads * cols_here]
        blocks = [own_part.reshape(local_heads, cols_here, cols_here)]
        for index, tile in enumerate(tiles):
            packed = tile[0].reshape(pairs, cols_here, 2, part_cols)
            packed = packed[:, :, ::-1] if index % CHUNKS % 2 == 1 else packed
            packed = jnp.transpose(packed, (0, 2, 1, 3))
            blocks.append(packed.reshape(local_heads, cols_here, part_cols))
        logits = jnp.concatenate(blocks, axis=2)
        share = lax.psum_scatter(logits, "depth", scatter_dimension=1, tiled=True)
        mask = jnp.concatenate(valid_tiles, axis=1)[None] > 0.5
        scaled = jnp.where(mask, share * lax.rsqrt(F32(head_width) * count), LOWEST)
        expo = jnp.where(mask, jnp.exp(scaled - jnp.max(scaled, axis=-1, keepdims=True)), 0.0)
        probs = (expo / jnp.sum(expo, axis=-1, keepdims=True)).astype(BF16)
        probs = lax.all_gather(probs, "depth", axis=1, tiled=True)
        probs = [probs.reshape(pairs, 2 * cols_here, total_cols)]

    piece = shape((part_rows, cols_here, local_width), BF16)
    mines, others = [], []
    for side in range(cores):
        gathers = len(probs) // 2
        outs = [piece]
        if gathers:
            outs.append(shape((pairs, 2 * cols_here, total_cols), BF16))
        mixed = call(
            functools.partial(
                mix_kernel,
                side=side,
                cores=cores,
                tiles=len(tiles),
                shards=gathers,
                heads=local_heads,
            ),
            outs,
            [spec()] * (len(probs) + 1 + len(remote_values)),
            flops=4 * part_rows * cols_here * total_cols * local_width,
        )(*probs, own_values, *remote_values)
        mines.append(mixed[0])
        probs = mixed[1:] if gathers else probs
        others.append([from_behind(mixed[0], "heads", k) for k in range(1, cores)])
    half = call(
        mine_kernel,
        shape((rows_here, cols_here, local_width), F32),
        [spec()] * (cores + 1),
        flops=2 * rows_here * cols_here * local_width * local_width,
    )(*mines, ordered)
    finished = []
    for side in range(cores - 1):
        finished.append(
            call(
                functools.partial(project_kernel, first=side * part_rows),
                piece,
                [spec()] * (cores + 2),
                flops=2 * part_rows * cols_here * width * local_width,
            )(live, half, *others[side], ordered)
        )
    return call(
        functools.partial(finish_kernel, cores=cores),
        shape((rows_here, cols_here, local_width), BF16),
        [spec()] * (2 * cores + 1),
        [
            pltpu.VMEM((part_rows, cols_here, local_width), BF16),
            pltpu.SemaphoreType.DMA((cores - 1 + part_rows,)),
        ],
        flops=2 * part_rows * cols_here * width * local_width,
        space=HBM,
    )(live, half, *others[cores - 1], ordered, *finished)


def solution(mesh):
    in_specs = (
        P(("groups", "depth"), "cols", None),
        P(),
        P(None, "heads"),
        P(None, "heads"),
        P(None, "heads"),
        P(None, "heads"),
        P(("groups", "depth")),
        P(("groups", "cols")),
    )
    out_specs = P(("groups", "depth"), "cols", "heads")

    return jax.shard_map(
        on_device, mesh=mesh, in_specs=in_specs, out_specs=out_specs, check_vma=False
    )
```

```python
import functools

import jax
import jax.numpy as jnp
from jax import lax
from jax.experimental import pallas as pl
from jax.experimental.pallas import tpu as pltpu
from jax.sharding import PartitionSpec as P

HEADS = 12
LANES = 128
CHUNKS = 2
SIZE = 2
LIMIT = 16 << 20
LOWEST = -1e30
PAD = 16


VMEM = pltpu.VMEM
SMEM = pltpu.SMEM
HBM = pltpu.HBM
BF16 = jnp.bfloat16
F32 = jnp.float32


def from_behind(value, axis, steps):
    count = lax.axis_size(axis)
    return lax.ppermute(value, axis, [(s, (s + steps) % count) for s in range(count)])


def spec(space=VMEM):
    return pl.BlockSpec(memory_space=space)


def call(kernel, out_shape, in_specs, scratch=(), flops=0, space=VMEM):
    single = not isinstance(out_shape, (list, tuple))
    shapes = [out_shape] if single else list(out_shape)
    nbytes = sum(s.size * s.dtype.itemsize for s in shapes)
    shapes = [space(s.shape, s.dtype) for s in shapes]
    fn = pl.pallas_call(
        kernel,
        out_shape=shapes,
        in_specs=in_specs,
        out_specs=[spec(space) for _ in shapes],
        scratch_shapes=list(scratch),
        compiler_params=pltpu.CompilerParams(vmem_limit_bytes=LIMIT),
        cost_estimate=pl.CostEstimate(flops=flops, transcendentals=0, bytes_accessed=2 * nbytes),
    )

    def run(*args):
        args = [
            arg
            if block.memory_space == SMEM
            else pltpu.with_memory_space_constraint(arg, block.memory_space)
            for arg, block in zip(args, in_specs, strict=True)
        ]
        out = fn(*args)
        return out[0] if single else out

    return run


def dot(left, right):
    return jnp.dot(left, right, preferred_element_type=F32)


def dot_t(left, right):
    return lax.dot_general(left, right, (((1,), (1,)), ((), ())), preferred_element_type=F32)


def normed_rows(rows, gain):
    values_f = rows.astype(F32)
    average = jnp.mean(values_f, axis=-1, keepdims=True)
    centred = values_f - average
    spread = jnp.mean(centred * centred, axis=-1, keepdims=True)
    return (centred * lax.rsqrt(spread + 1e-05) * gain).astype(BF16)


def first_kernel(rows_in, chunk, sems, *, part_cols):
    part_rows = chunk.shape[0] // part_cols
    begin = lax.axis_index("heads") * part_rows
    copies = []
    for r in range(part_rows):
        source = rows_in.at[begin + r, pl.ds(0, part_cols), :]
        target = chunk.at[pl.ds(r * part_cols, part_cols)]
        copies.append(pltpu.make_async_copy(source, target, sems.at[r]))
        copies[-1].start()
    for copy in copies:
        copy.wait()


def load_kernel(valid, rows_in, resident, *rest, part_cols):
    lasts, flags, sems = rest[:-2], rest[-2], rest[-1]
    rows_here, cols, _ = resident.shape
    some = lasts[-1].shape[0] // part_cols
    begin = lax.axis_index("heads") * some * len(lasts)
    first = pltpu.make_async_copy(valid, flags, sems.at[rows_here + some * len(lasts)])
    first.start()
    copies = []
    for r in range(some * len(lasts)):
        source = rows_in.at[begin + r, pl.ds(cols - part_cols, part_cols), :]
        target = lasts[r // some].at[pl.ds(r % some * part_cols, part_cols)]
        copies.append(pltpu.make_async_copy(source, target, sems.at[rows_here + r]))
    for r in range(rows_here):
        copies.append(pltpu.make_async_copy(rows_in.at[r], resident.at[r], sems.at[r]))
    for copy in copies:
        copy.start()
    first.wait()
    tail = some * part_cols
    lasts[0][tail:, :] = jnp.zeros((PAD, lasts[0].shape[1]), BF16)
    lasts[0][tail:, 0:cols] = jnp.broadcast_to(flags[...].astype(F32), (PAD, cols)).astype(BF16)
    for copy in copies:
        copy.wait()


def side_by_side(block, first, cols, pair):
    at = slice(pair * LANES, (pair + 1) * LANES)
    pieces = [block[(first + r) * cols : (first + r + 1) * cols, at] for r in range(SIZE)]
    return jnp.concatenate(pieces, axis=1)


def write_shards(total, shards, depth_index):
    slots, cols, _ = total.shape
    count = len(shards)
    part = cols // count
    for k, shard in enumerate(shards):
        begin = lax.bitwise_xor(depth_index, k) * part if count > 1 else 0
        for slot in range(slots):
            rows = total[slot, pl.ds(pl.multiple_of(begin, part), part), :]
            shard[slot * part : (slot + 1) * part, :] = rows


def own_kernel(live, rows_in, gain, w_query, w_key, *rest, shards):
    normed_out, query_out = rest[0], rest[1]
    outs = rest[2 : 2 + shards]
    keys, total = rest[2 + shards :]
    groups, pairs = query_out.shape[0], query_out.shape[1]
    _, cols, width = rows_in.shape
    low = lax.broadcasted_iota(jnp.int32, (cols, LANES), 1) < LANES // 2
    zero = jnp.zeros((cols, LANES), BF16)
    local = w_query.shape[1]
    weights = jnp.concatenate([w_query[...], w_key[...]], axis=1)
    for g in range(groups):
        rows = rows_in[g * SIZE : (g + 1) * SIZE].reshape(SIZE * cols, width)
        normed = normed_rows(rows, gain[...])
        normed_out[g] = normed
        both_sides = dot(normed, weights)
        query, key = both_sides[:, :local], both_sides[:, local:].astype(BF16)
        for r in range(SIZE):
            scale = live[g * SIZE + r : g * SIZE + r + 1, :]
            for p in range(pairs):
                both = query[r * cols : (r + 1) * cols, p * LANES : (p + 1) * LANES]
                both = (both * scale).astype(BF16)
                at = slice(r * LANES, (r + 1) * LANES)
                query_out[g, p, 0:cols, at] = jnp.where(low, both, zero)
                query_out[g, p, cols : 2 * cols, at] = jnp.where(low, zero, both)
        for p in range(pairs):
            keys[g, p] = side_by_side(key, 0, cols, p)
    for p in range(pairs):
        score = dot_t(query_out[0, p], keys[0, p])
        for g in range(1, groups):
            score = score + dot_t(query_out[g, p], keys[g, p])
        total[2 * p] = score[:cols]
        total[2 * p + 1] = score[cols:]
    write_shards(total, outs, lax.axis_index("depth"))
    real = jnp.sum(live[...], axis=0, keepdims=True)
    for out in outs:
        out[out.shape[0] - 8 :, :] = jnp.broadcast_to(real, (8, LANES))


def value_kernel(*refs, cores, cols):
    parts = len(refs) - 2
    normed, w_value, values = refs[:parts], refs[parts], refs[parts + 1]
    _, inner, pairs, _, _ = values.shape
    each = inner * cores // parts
    for n in range(parts):
        value = dot(normed[n][...], w_value[...]).astype(BF16)
        for g in range(each):
            for p in range(pairs):
                block = side_by_side(value, g * SIZE, cols, p)
                values[n % cores, n // cores * each + g, p] = block


def own_value_kernel(normed, w_value, values, *, cols):
    for g in range(values.shape[0]):
        value = dot(normed[g], w_value[...]).astype(BF16)
        for p in range(values.shape[1]):
            values[g, p] = side_by_side(value, 0, cols, p)


def remote_kernel(part, gain, w_key, query, *rest, step, steps, chunk, part_cols, cores, shards):
    if step > 0:
        before, rest = rest[0], rest[1:]
    normed_out, rest = rest[0], rest[1:]
    last = step + 1 == steps
    used = normed_out.shape[0]
    rows, cols = used // part_cols, part_cols
    pairs, full = query.shape[1], query.shape[2] // 2
    normed = normed_rows(part[0:used, :], gain[...])
    normed_out[...] = normed
    key = dot(normed, w_key[...]).astype(BF16)
    total = rest[shards] if last else rest[0]
    inner = rows // SIZE
    source = lax.rem(lax.axis_index("heads") + cores - step % cores, cores)
    base = source * (steps // cores) * inner + step // cores * inner
    low = lax.broadcasted_iota(jnp.int32, (full, LANES), 1) < LANES // 2
    for p in range(pairs):
        score = before[p] if step > 0 else None
        whole = None
        for g in range(inner):
            one = side_by_side(key, g * SIZE, cols, p)
            twice = jnp.concatenate([one, one], axis=0)
            extra = dot_t(query[base + g, p], twice)
            whole = extra if whole is None else whole + extra
        left, right = whole[:full], whole[full:]
        if chunk % 2 == 1:
            left, right = right, left
        packed = jnp.where(low, left, right)
        total[p] = packed if score is None else score + packed
    if last:
        write_shards(total, rest[:shards], lax.axis_index("depth"))


def added(pieces):
    total = pieces[0][...]
    for piece in pieces[1:]:
        total = total + piece[...]
    return total


def diagonal(rows):
    row = lax.broadcasted_iota(jnp.int32, (rows, LANES), 0)
    return row == lax.broadcasted_iota(jnp.int32, (rows, LANES), 1)


def low_lanes(rows):
    return lax.broadcasted_iota(jnp.int32, (rows, LANES), 1) < LANES // 2


def half_mask(valid, half, rows):
    flags = valid[...]
    turned = pltpu.roll(flags, LANES // 2, 1)
    low = low_lanes(1)
    both = jnp.where(low, flags, turned) if half == 0 else jnp.where(low, turned, flags)
    return jnp.broadcast_to(both > 0.5, (rows, LANES))


def row_max(block):
    return jnp.max(block, axis=-1, keepdims=True)


def row_sum(block):
    return jnp.sum(block, axis=-1, keepdims=True)


def own_soft_kernel(*rest, shards, offsets, heads, head_width):
    valid, rest = rest[: 1 + offsets], rest[1 + offsets :]
    probs, stats = rest[-2:]
    sums = [added(rest[t * shards : (t + 1) * shards]) for t in range(1 + offsets)]
    rows = stats.shape[1]
    part = rows // heads
    factor = lax.rsqrt(F32(head_width) * sums[0][rows : rows + 1, 0:1])
    mask = jnp.broadcast_to(valid[0][...] > 0.5, (part, LANES))
    halves = [half_mask(valid[1 + o], 0, part) for o in range(offsets)]
    low = low_lanes(part)
    for p in range(heads // 2):
        at = slice(p * part, (p + 1) * part)
        near = []
        for o in range(offsets):
            near.append(jnp.where(halves[o], sums[1 + o][at] * factor, LOWEST))
        highest = functools.reduce(jnp.maximum, near)
        tops, wholes = [], []
        for h in (2 * p, 2 * p + 1):
            mine = slice(h * part, (h + 1) * part)
            side = low if h % 2 == 0 else jnp.logical_not(low)
            scaled = jnp.where(mask, sums[0][mine] * factor, LOWEST)
            top = row_max(jnp.maximum(scaled, jnp.where(side, highest, LOWEST)))
            expo = jnp.where(mask, jnp.exp(scaled - top), 0.0)
            probs[mine, :] = expo.astype(BF16)
            tops.append(top)
            wholes.append(expo)
        top = jnp.where(low, tops[0], tops[1])
        mass = jnp.zeros((part, LANES), F32)
        for o in range(offsets):
            expo = jnp.where(halves[o], jnp.exp(near[o] - top), 0.0)
            begin = rows + (o * heads // 2 + p) * part
            probs[begin : begin + part, :] = expo.astype(BF16)
            mass = mass + expo
        for h in (2 * p, 2 * p + 1):
            mine = slice(h * part, (h + 1) * part)
            side = low if h % 2 == 0 else jnp.logical_not(low)
            whole = row_sum(wholes[h % 2] + jnp.where(side, mass, 0.0))
            stats[0, mine, :] = jnp.broadcast_to(tops[h % 2], (part, LANES))
            stats[1, mine, :] = jnp.broadcast_to(whole, (part, LANES))
            stats[2, mine, :] = jnp.broadcast_to(factor, (part, LANES))


def last_soft_kernel(*rest, shards, offsets, heads):
    valid, stats, probs = rest[:offsets], rest[offsets], rest[-1]
    rest = rest[offsets + 1 : -1]
    sums = [added(rest[t * shards : (t + 1) * shards]) for t in range(offsets)]
    part = stats.shape[1] // heads
    low = low_lanes(part)
    halves = [half_mask(valid[o], 1, part) for o in range(offsets)]
    kept = diagonal(part)
    lines = []
    for p in range(heads // 2):
        at = slice(p * part, (p + 1) * part)
        factor = stats[2, 2 * p * part : (2 * p + 1) * part, :]
        far = [jnp.where(halves[o], sums[o][at] * factor, LOWEST) for o in range(offsets)]
        highest = functools.reduce(jnp.maximum, far)
        tops, shifts = [], []
        for h in (2 * p, 2 * p + 1):
            old = stats[0, h * part : (h + 1) * part, :]
            side = jnp.logical_not(low) if h % 2 == 0 else low
            top = jnp.maximum(old, row_max(jnp.where(side, highest, LOWEST)))
            tops.append(top)
            shifts.append(jnp.exp(old - top))
        top = jnp.where(low, tops[1], tops[0])
        expo = [jnp.where(halves[o], jnp.exp(far[o] - top), 0.0) for o in range(offsets)]
        mass = functools.reduce(jnp.add, expo)
        wholes = []
        for h in (2 * p, 2 * p + 1):
            side = jnp.logical_not(low) if h % 2 == 0 else low
            own = stats[1, h * part : (h + 1) * part, :]
            whole = shifts[h % 2] * own + row_sum(jnp.where(side, mass, 0.0))
            wholes.append(whole)
            block = jnp.where(kept, shifts[h % 2] / whole, 0.0)
            lines.append(jnp.sum(block, axis=0, keepdims=True))
        whole = jnp.where(low, wholes[1], wholes[0])
        for o in range(offsets):
            begin = (o * heads // 2 + p) * part
            probs[begin : begin + part, :] = (expo[o] / whole).astype(BF16)
    lines = jnp.concatenate(lines + [jnp.zeros((8 - heads, LANES), F32)], axis=0)
    coarse = lines.astype(BF16).astype(F32)
    tail = jnp.concatenate([coarse, lines - coarse], axis=0)
    probs[probs.shape[0] - PAD :, :] = tail.astype(BF16)


def collect(owns, others, probs, heads):
    blocks = probs.shape[2] // LANES
    cols = probs.shape[1] // 2
    part = (others[0].shape[0] - PAD) // ((blocks - 1) * heads // 2)
    kept = diagonal(part)
    low = low_lanes(part)
    for k in range(len(owns)):
        begin = lax.bitwise_xor(lax.axis_index("depth"), k) * part
        tail = others[k][others[k].shape[0] - PAD :, :].astype(F32)
        lines = tail[0:8] + tail[8:16]
        for head in range(heads):
            at = pl.ds(pl.multiple_of(head % 2 * cols + begin, part), part)
            line = jnp.where(kept, jnp.broadcast_to(lines[head : head + 1], (part, LANES)), 0.0)
            scale = row_sum(line)
            own = owns[k][head * part : (head + 1) * part, :].astype(F32) * scale
            probs[head // 2, at, 0:LANES] = own.astype(BF16)
            for o in range(blocks - 1):
                first = (o * heads // 2 + head // 2) * part
                near = owns[k][heads * part + first : heads * part + first + part, :]
                near = near.astype(F32) * scale
                far = others[k][first : first + part, :].astype(F32)
                if head % 2 == 0:
                    both = jnp.where(low, near, far)
                else:
                    both = pltpu.roll(jnp.where(low, far, near), LANES // 2, 1)
                probs[head // 2, at, (1 + o) * LANES : (2 + o) * LANES] = both.astype(BF16)


def mix_kernel(*rest, side, cores, tiles, shards, heads):
    if shards:
        rest, probs = rest[:-1], rest[-1]
        collect(rest[:shards], rest[shards : 2 * shards], probs, heads)
        rest = rest[2 * shards :]
    else:
        probs, rest = rest[0], rest[1:]
    own, remote, out = rest[0], rest[1 : 1 + tiles], rest[1 + tiles]
    _, pairs, cols, lanes = own.shape
    inner = own.shape[0] // cores
    low = jnp.concatenate([low_lanes(cols)] * (lanes // LANES), axis=1)
    step = lax.rem(lax.axis_index("heads") + cores - side, cores)
    for g in range(inner):
        for p in range(pairs):
            blocks = [own[side * inner + g, p]]
            blocks += [block[step, g, p] for block in remote]
            mixed = dot(probs[p], jnp.concatenate(blocks, axis=0))
            picked = jnp.where(low, mixed[:cols], mixed[cols:]).astype(BF16)
            for r in range(SIZE):
                at = slice(r * LANES, (r + 1) * LANES)
                out[g * SIZE + r, :, p * LANES : (p + 1) * LANES] = picked[:, at]


def order_kernel(w_out, ordered, *, cores):
    local = w_out.shape[0] // cores
    for k in range(cores):
        source = lax.rem(lax.axis_index("heads") + cores - k, cores)
        rows = w_out[pl.ds(pl.multiple_of(source * local, local), local), :]
        ordered[k * local : (k + 1) * local, :] = rows


def mine_kernel(*rest):
    parts, weights, out = rest[:-2], rest[-2], rest[-1]
    size, cols, local = parts[0].shape
    for side, part in enumerate(parts):
        rows = part[...].reshape(size * cols, local)
        total = dot(rows, weights[0:local, :])
        out[side * size : (side + 1) * size] = total.reshape(size, cols, local)


def projected(live, half, parts, weights, begin, first):
    cols, local = parts[0].shape[1], parts[0].shape[2]
    blocks = [part[begin : begin + SIZE].reshape(SIZE * cols, local) for part in parts]
    block = jnp.concatenate(blocks, axis=1) if len(blocks) > 1 else blocks[0]
    at = first + begin
    total = dot(block, weights[local:, :]) + half[at : at + SIZE].reshape(SIZE * cols, local)
    results = []
    for r in range(SIZE):
        scale = live[at + r : at + r + 1, :]
        scale = jnp.concatenate([scale] * (local // LANES), axis=1)
        results.append((total[r * cols : (r + 1) * cols] * scale).astype(BF16))
    return results


def project_kernel(live, half, *rest, first):
    parts, weights, out = rest[:-2], rest[-2], rest[-1]
    for begin in range(0, out.shape[0], SIZE):
        for r, rows in enumerate(projected(live, half, parts, weights, begin, first)):
            out[begin + r] = rows


def finish_kernel(live, half, *rest, cores):
    parts, weights, ready = rest[: cores - 1], rest[cores - 1], rest[cores:-3]
    out, buffer, sems = rest[-3:]
    size = buffer.shape[0]
    copies = []
    for k, done in enumerate(ready):
        for r in range(size):
            target, sem = out.at[k * size + r], sems.at[k * size + r]
            copies.append(pltpu.make_async_copy(done.at[r], target, sem))
            copies[-1].start()
    first = len(ready) * size
    for begin in range(0, size, SIZE):
        for r, rows in enumerate(projected(live, half, parts, weights, begin, first)):
            row = begin + r
            buffer[row] = rows
            target = out.at[first + row]
            copies.append(pltpu.make_async_copy(buffer.at[row], target, sems.at[first + row]))
            copies[-1].start()
    for copy in copies:
        copy.wait()


def on_device(alignment, norm_gain, w_query, w_key, w_value, w_out, row_mask, col_valid):
    rows_here, cols_here, width = alignment.shape
    local_width = w_query.shape[1]
    head_width = width // HEADS
    local_heads = local_width // head_width
    pairs = local_heads // 2
    offsets = lax.axis_size("cols") - 1
    depth = lax.axis_size("depth")
    cores = lax.axis_size("heads")
    part_rows = rows_here // cores
    inner = part_rows // SIZE
    groups = rows_here // SIZE
    part_cols = cols_here // CHUNKS
    direct = depth in (2, 4, 8) and cols_here % (16 * depth) == 0
    shards = depth if direct else 1
    part = cols_here // shards
    lanes = SIZE * LANES
    total_cols = (1 + offsets) * cols_here
    shape = jax.ShapeDtypeStruct
    gain = norm_gain[None, :]
    live = jnp.broadcast_to(row_mask.astype(F32)[:, None], (rows_here, LANES))

    first = call(
        functools.partial(first_kernel, part_cols=part_cols),
        shape((part_rows * part_cols, width), BF16),
        [spec(HBM)],
        [pltpu.SemaphoreType.DMA((part_rows,))],
    )(alignment)
    sent = {(0, 0): first}
    spans = [1] * CHUNKS
    some = part_rows // spans[-1] * part_cols
    resident, *lasts = call(
        functools.partial(load_kernel, part_cols=part_cols),
        [shape((rows_here, cols_here, width), BF16), shape((some + PAD, width), BF16)]
        + [shape((some, width), BF16)] * (spans[-1] - 1),
        [spec(HBM), spec(HBM)],
        [
            pltpu.VMEM((1, cols_here), jnp.int32),
            pltpu.SemaphoreType.DMA((part_rows + rows_here + 1,)),
        ],
    )(col_valid[None, :], alignment)
    for m, block in enumerate(lasts):
        sent[CHUNKS - 1, m] = block
    arrived = {}
    for offset in range(1, offsets + 1):
        for (c, m), block in sent.items():
            mine = from_behind(block, "cols", offset)
            arrived[offset, c, m] = [mine] + [
                from_behind(mine, "heads", k) for k in range(1, cores)
            ]

    def exchange(values):
        received = [values[0]]
        for k in range(1, shards):
            swapped = [(source, source ^ k) for source in range(depth)]
            received.append(lax.ppermute(values[k], "depth", swapped))
        return received

    own = call(
        functools.partial(own_kernel, shards=shards),
        [
            shape((groups, SIZE * cols_here, width), BF16),
            shape((groups, pairs, 2 * cols_here, lanes), BF16),
        ]
        + [shape((local_heads * part + 8, cols_here), F32)] * shards,
        [spec()] * 5,
        [
            pltpu.VMEM((groups, pairs, cols_here, lanes), BF16),
            pltpu.VMEM((local_heads, cols_here, cols_here), F32),
        ],
        flops=4 * rows_here * cols_here * width * local_width,
    )(live, resident, gain, w_query, w_key)
    normed, query, own_sums = own[0], own[1], exchange(own[2:])

    own_values = call(
        functools.partial(own_value_kernel, cols=cols_here),
        shape((groups, pairs, cols_here, lanes), BF16),
        [spec()] * 2,
        flops=2 * rows_here * cols_here * width * local_width,
    )(normed, w_value)
    ordered = call(
        functools.partial(order_kernel, cores=cores), shape(w_out.shape, BF16), [spec()]
    )(w_out)

    tiles, remote_values = [], []
    for offset in range(1, offsets + 1):
        for c in range(CHUNKS):
            before, rows_of = [], []
            steps = spans[c] * cores
            used = part_rows // spans[c] * part_cols
            for n in range(steps):
                m, k = divmod(n, cores)
                outs = [shape((used, width), BF16)]
                scratch = []
                if n + 1 == steps:
                    outs += [shape((pairs * part, LANES), F32)] * shards
                    scratch = [pltpu.VMEM((pairs, cols_here, LANES), F32)]
                else:
                    outs += [shape((pairs, cols_here, LANES), F32)]
                result = call(
                    functools.partial(
                        remote_kernel,
                        step=n,
                        steps=steps,
                        chunk=c,
                        part_cols=part_cols,
                        cores=cores,
                        shards=shards,
                    ),
                    outs,
                    [spec()] * (4 + len(before)),
                    scratch,
                    flops=2 * used * width * local_width,
                )(arrived[offset, c, m][k], gain, w_key, query, *before)
                rows_of.append(result[0])
                before = [result[1]]
            tiles.append(exchange(result[1:]))
            remote_values.append(
                call(
                    functools.partial(value_kernel, cores=cores, cols=part_cols),
                    shape((cores, inner, pairs, part_cols, lanes), BF16),
                    [spec()] * (steps + 1),
                    flops=2 * cores * part_rows * part_cols * width * local_width,
                )(*rows_of, w_value)
            )

    valid_tiles = [col_valid.astype(BF16)[None, :]]
    for offset in range(1, offsets + 1):
        valid_tiles.append(arrived[offset, CHUNKS - 1, 0][0][-PAD : 1 - PAD, :cols_here])
    if direct:
        valid = [tile.astype(F32) for tile in valid_tiles]
        rows = local_heads * part
        far_rows = offsets * pairs * part
        early = [piece for tile in tiles[0::CHUNKS] for piece in tile]
        late = [piece for tile in tiles[1::CHUNKS] for piece in tile]
        own_probs, stats = call(
            functools.partial(
                own_soft_kernel,
                shards=shards,
                offsets=offsets,
                heads=local_heads,
                head_width=head_width,
            ),
            [shape((rows + far_rows, LANES), BF16), shape((3, rows, LANES), F32)],
            [spec()] * ((1 + offsets) * (1 + shards)),
            flops=1000000,
        )(*valid, *own_sums, *early)
        own_probs = exchange([own_probs] * shards)
        probs = call(
            functools.partial(
                last_soft_kernel, shards=shards, offsets=offsets, heads=local_heads
            ),
            shape((far_rows + PAD, LANES), BF16),
            [spec()] * (1 + offsets * (1 + shards)),
            flops=1000000,
        )(*valid[1:], stats, *late)
        probs = exchange([probs] * shards)
        probs = own_probs + probs
    else:
        count = lax.psum(jnp.sum(row_mask.astype(F32)), "depth")
        own_part = own_sums[0][: local_heads * cols_here]
        blocks = [own_part.reshape(local_heads, cols_here, cols_here)]
        for index, tile in enumerate(tiles):
            packed = tile[0].reshape(pairs, cols_here, 2, part_cols)
            packed = packed[:, :, ::-1] if index % CHUNKS % 2 == 1 else packed
            packed = jnp.transpose(packed, (0, 2, 1, 3))
            blocks.append(packed.reshape(local_heads, cols_here, part_cols))
        logits = jnp.concatenate(blocks, axis=2)
        share = lax.psum_scatter(logits, "depth", scatter_dimension=1, tiled=True)
        mask = jnp.concatenate(valid_tiles, axis=1)[None] > 0.5
        scaled = jnp.where(mask, share * lax.rsqrt(F32(head_width) * count), LOWEST)
        expo = jnp.where(mask, jnp.exp(scaled - jnp.max(scaled, axis=-1, keepdims=True)), 0.0)
        probs = (expo / jnp.sum(expo, axis=-1, keepdims=True)).astype(BF16)
        probs = lax.all_gather(probs, "depth", axis=1, tiled=True)
        probs = [probs.reshape(pairs, 2 * cols_here, total_cols)]

    piece = shape((part_rows, cols_here, local_width), BF16)
    mines, others = [], []
    for side in range(cores):
        gathers = len(probs) // 2
        outs = [piece]
        if gathers:
            outs.append(shape((pairs, 2 * cols_here, total_cols), BF16))
        mixed = call(
            functools.partial(
                mix_kernel,
                side=side,
                cores=cores,
                tiles=len(tiles),
                shards=gathers,
                heads=local_heads,
            ),
            outs,
            [spec()] * (len(probs) + 1 + len(remote_values)),
            flops=4 * part_rows * cols_here * total_cols * local_width,
        )(*probs, own_values, *remote_values)
        mines.append(mixed[0])
        probs = mixed[1:] if gathers else probs
        others.append([from_behind(mixed[0], "heads", k) for k in range(1, cores)])
    half = call(
        mine_kernel,
        shape((rows_here, cols_here, local_width), F32),
        [spec()] * (cores + 1),
        flops=2 * rows_here * cols_here * local_width * local_width,
    )(*mines, ordered)
    finished = []
    for side in range(cores - 1):
        finished.append(
            call(
                functools.partial(project_kernel, first=side * part_rows),
                piece,
                [spec()] * (cores + 2),
                flops=2 * part_rows * cols_here * width * local_width,
            )(live, half, *others[side], ordered)
        )
    return call(
        functools.partial(finish_kernel, cores=cores),
        shape((rows_here, cols_here, local_width), BF16),
        [spec()] * (2 * cores + 1),
        [
            pltpu.VMEM((part_rows, cols_here, local_width), BF16),
            pltpu.SemaphoreType.DMA((rows_here,)),
        ],
        flops=2 * part_rows * cols_here * width * local_width,
        space=HBM,
    )(live, half, *others[cores - 1], ordered, *finished)


def solution(mesh):
    in_specs = (
        P(("groups", "depth"), "cols", None),
        P(),
        P(None, "heads"),
        P(None, "heads"),
        P(None, "heads"),
        P(None, "heads"),
        P(("groups", "depth")),
        P(("groups", "cols")),
    )
    out_specs = P(("groups", "depth"), "cols", "heads")

    return jax.shard_map(
        on_device, mesh=mesh, in_specs=in_specs, out_specs=out_specs, check_vma=False
    )
```
